512 devices in a mesh: row: 32 (over x, y), col: 16 (over z, core).
Axes of the slice: x: 4, y: 8, z: 8, core: 2. Of those that a mesh axis runs over, the one named last changes fastest.
Arguments:
- item_factors: bfloat16 [64, 2048, 256], P('col', 'row'), may hold values from -1 to 1
- tile_counts: int32 [64], P('col'), may hold values from 1024 to 2048, as said below
- observed_tiles: int32 [32, 32], P('row', 'col'), may hold values from 0 to 3, as said below
- mask_words: int32 [4096, 32, 256], P('row', 'col'), may hold values from 0 to 255
- confidence: float32 [4096], P('row'), may hold values from 1 to 40
- previous: bfloat16 [4096, 256], P('row'), may hold values from -6 to 6
Outputs:
- user_factors: float32 [4096, 256], P('row')
The draws below stay inside these ranges and needn't reach their ends.
Inputs may be any that keep to these rules, and one draw needn't show every extreme that they name: `tile_counts`: a tile's slots at and past its count are padding; some tile of the draw has all 2048 slots valid. `observed_tiles`: the 2 entries of one user block and one column group are distinct.
All inputs are finite; a program needn't handle non-finite values.
Results may differ from the reference program's by a relative error of at most 0.0013.
The reference program's roundings to bfloat16 on the way (of `seen` and `weights`) count: a program that leaves them out, or rounds other values in their place, can miss the bound.
Values may be sent and summed in bfloat16 or wider, within the bound.
A program may use at most 64 MiB of HBM per device.

```python
import math
import jax
import jax.numpy as jnp
from jax import lax

R = 256
TILE = 2048
U_DEV = 128
TILES_COL = 4
OBS = 2
ITERS = 3
USERS = 4096
BLOCKS = 32
GROUPS = 16
TILES = 64
WORDS = 256


def draw_item_factors(key, part):
    key_scale = jax.random.fold_in(key, 11)
    key_base = jax.random.fold_in(key, 12)
    scales = jnp.exp(jax.random.uniform(key_scale, (R,), jnp.float32, jnp.log(0.1), 0.0))
    base = jnp.clip(jax.random.normal(key_base, (TILES, TILE, R), jnp.float32), -4.0, 4.0)
    return (base * scales / jnp.sqrt(jnp.float32(TILES * TILE))).astype(jnp.bfloat16)


def draw_tile_counts(key, part):
    key_count = jax.random.fold_in(key, 21)
    key_full = jax.random.fold_in(key, 22)
    counts = jax.random.randint(key_count, (TILES,), TILE // 2, TILE + 1, jnp.int32)
    chosen = jax.random.randint(key_full, (), 0, TILES, jnp.int32)
    return jnp.where(jnp.arange(TILES, dtype=jnp.int32) == chosen, TILE, counts).astype(jnp.int32)


def draw_observed_tiles(key, part):
    keys = jax.random.split(jax.random.fold_in(key, 31), BLOCKS * GROUPS)
    picks = jax.vmap(lambda key_one: jax.random.permutation(key_one, TILES_COL)[:OBS])(keys)
    return picks.reshape(BLOCKS, GROUPS * OBS).astype(jnp.int32)


def with_ends(values, rng, smallest, top_value):
    shape = values.shape
    index_at = [jax.random.randint(jax.random.fold_in(rng, axis), (), 0, shape[axis]) for axis in range(len(shape))]
    values = values.at[tuple(index_at)].set(smallest)
    longest = shape.index(max(shape))
    index_at[longest] = (index_at[longest] + 1) % shape[longest]
    return values.at[tuple(index_at)].set(top_value)


def block_scale(rng, dims, shards, low, top_value):
    def one(position, parts):
        steps = jax.random.uniform(jax.random.fold_in(jax.random.fold_in(rng, 6), position), (parts,), jnp.float32, low / len(shards), top_value / len(shards))
        return jnp.repeat(jnp.exp(steps), dims[position] // parts).reshape((-1,) + (1,) * (len(dims) - position - 1))

    gain = one(*shards[0])
    for cut in shards[1:]:
        gain = gain * one(*cut)
    return gain


def bell_draw(own_key, dims, width, most, shards=(), kind=jnp.bfloat16):
    values = width * jax.random.normal(own_key, dims, jnp.float32)
    if shards:
        values = values * block_scale(own_key, dims, shards, -0.22, 0.18)
    return jnp.clip(values, -most, most).astype(kind)


def setup_inputs(seed: int = 0) -> dict:
    streams_of = jax.random.split(jax.random.key(seed), 7)
    return {
        "item_factors": draw_item_factors(jax.random.fold_in(streams_of[6], 71), 0),
        "tile_counts": draw_tile_counts(jax.random.fold_in(streams_of[6], 71), 0),
        "observed_tiles": draw_observed_tiles(jax.random.fold_in(streams_of[6], 71), 0),
        "mask_words": with_ends(jax.random.randint(streams_of[3], (USERS, GROUPS * OBS, WORDS), 0, 256), jax.random.fold_in(streams_of[3], 1), 0, 255).astype(jnp.int32),
        "confidence": jnp.clip(jnp.exp(math.log(40.0) - 3.6888795 * jax.random.uniform(streams_of[4], (USERS,), jnp.float32) ** block_scale(streams_of[4], (USERS,), ((0, 32),), -0.2, 0.2)), 1.0, 40.0),
        "previous": bell_draw(streams_of[5], (USERS, R), 1.0, 6.0, ((0, 32),)),
    }


ridge_weight = 0.1


def unpack_bits(words):
    shifts = jnp.arange(8, dtype=jnp.int32)
    bits = jnp.right_shift(words[..., None], shifts) & 1
    return bits.reshape(words.shape[:-1] + (words.shape[-1] * 8,))


def reference(item_factors, tile_counts, observed_tiles, mask_words, confidence, previous):
    slot_index = jnp.arange(TILE, dtype=jnp.int32)

    def add_gram(total, inputs):
        tile_rows, count_now = inputs
        masked = jnp.where((slot_index < count_now)[:, None], tile_rows, jnp.zeros_like(tile_rows))
        return total + jnp.dot(masked.T, masked, preferred_element_type=jnp.float32), None

    gram, _ = lax.scan(add_gram, jnp.zeros((R, R), jnp.float32), (item_factors, tile_counts))
    slots = GROUPS * OBS

    def solve_block(inputs):
        prev_rows, alpha, words, observed = inputs
        tile_ids = ((jnp.arange(slots, dtype=jnp.int32) // OBS) * TILES_COL + observed).astype(jnp.int32)
        tiles = item_factors[tile_ids]
        valid = (slot_index[None, :] < tile_counts[tile_ids][:, None]).astype(jnp.int32)
        seen = (unpack_bits(words) * valid[None]).astype(jnp.bfloat16)
        seen = jnp.transpose(seen, (1, 0, 2))

        def rhs_add(total, pair):
            return total + jnp.dot(pair[1], pair[0], preferred_element_type=jnp.float32), None

        rhs_sum, _ = lax.scan(rhs_add, jnp.zeros((U_DEV, R), jnp.float32), (tiles, seen))
        rhs = (1.0 + alpha)[:, None] * rhs_sum

        def apply_op(vector):
            rounded = vector.astype(jnp.bfloat16)

            def term_add(total, pair):
                tile_rows, seen_now = pair
                scores = jnp.dot(rounded, tile_rows.T, preferred_element_type=jnp.float32)
                weights = (alpha[:, None] * seen_now.astype(jnp.float32) * scores).astype(jnp.bfloat16)
                return total + jnp.dot(weights, tile_rows, preferred_element_type=jnp.float32), None

            summed, _ = lax.scan(term_add, jnp.zeros((U_DEV, R), jnp.float32), (tiles, seen))
            return jnp.dot(vector, gram, precision=lax.Precision.HIGHEST) + ridge_weight * vector + summed

        solution = prev_rows.astype(jnp.float32)
        residual = rhs - apply_op(solution)
        direction = residual
        norm_now = jnp.sum(residual * residual, axis=1)
        for iteration in range(ITERS):
            image = apply_op(direction)
            step_size = norm_now / jnp.sum(direction * image, axis=1)
            solution = solution + step_size[:, None] * direction
            residual = residual - step_size[:, None] * image
            norm_next = jnp.sum(residual * residual, axis=1)
            direction = residual + (norm_next / norm_now)[:, None] * direction
            norm_now = norm_next
        return solution

    result = lax.map(solve_block, (previous.reshape(BLOCKS, U_DEV, R), confidence.reshape(BLOCKS, U_DEV),
                                   mask_words.reshape(BLOCKS, U_DEV, slots, WORDS), observed_tiles))
    return result.reshape(USERS, R)
```

```python
import functools
import heapq

import jax
import jax.numpy as jnp
from jax import lax
from jax.experimental import pallas as pl
from jax.experimental.pallas import tpu as pltpu
from jax.sharding import PartitionSpec as P

R = 256
HALF = 128
OBS = 2
ITERS = 3
TILES_COL = 4
UNITS = 2 * TILES_COL
RIDGE = 0.1
NX, NY, NZ = 4, 8, 8
A_UNITS = 5
MESH = pl.DeviceIdType.MESH


def plan(rows):
    a_us, b_us = 1.76 * rows / 64, 1.06 * rows / 64
    free = {}
    heap = []
    events = []
    order = []
    tick = [0]

    def send(now, piece):
        kind, axis, sign, hops, dx, dy, lo, hi = piece
        link = (axis, sign)
        start = max(now, free.get(link, 0.0))
        cost = (a_us if kind == "A" else b_us) * (hi - lo) / rows
        free[link] = start + cost
        tick[0] += 1
        heapq.heappush(heap, (start + cost + 1.6, tick[0], piece))
        order.append(piece)

    def spread(now, kind, axis, dx, dy, lo, hi):
        for sign in (1, -1):
            send(now, (kind, axis, sign, 1, dx, dy, lo, hi))

    spread(0.0, "A", "y", 0, 0, 0, rows)
    spread(0.0, "B", "x", 0, 0, 0, rows)
    spread(0.0, "A", "x", 0, 0, 0, rows)
    spread(0.0, "B", "y", 0, 0, 0, rows)
    events.append((None, list(order), 0.0))
    while heap:
        now, _, piece = heapq.heappop(heap)
        order.clear()
        kind, axis, sign, hops, dx, dy, lo, hi = piece
        ring = NX if axis == "x" else NY
        if axis == "x":
            dx = dx + sign
        else:
            dy = dy + sign
        if hops < ring // 2:
            middle = (lo + hi) // 2
            if hops < ring // 2 - 1:
                send(now, (kind, axis, sign, hops + 1, dx, dy, lo, hi))
            elif sign == 1:
                send(now, (kind, axis, sign, hops + 1, dx, dy, lo, middle))
            else:
                send(now, (kind, axis, sign, hops + 1, dx, dy, middle, hi))
        if kind == "A" and axis == "y":
            spread(now, "A", "x", dx, dy, lo, hi)
        if kind == "B" and axis == "x":
            spread(now, "B", "y", dx, dy, lo, hi)
        events.append((piece, list(order), now))
    return events


def kernel(
    counts,
    observed,
    conf_in,
    prev_in,
    words_in,
    item_hbm,
    out_ref,
    buf,
    picked,
    cs,
    seen,
    part,
    heard,
    vectors,
    gram,
    load_sem,
    send_sem,
    recv_sem,
    sum_send,
    sum_recv,
    vec_send,
    vec_recv,
    *,
    events,
    rows,
):
    me_row = lax.axis_index("row")
    me_col = lax.axis_index("col")
    my_x, my_y = me_row // NY, me_row % NY
    my_z, my_core = me_col // 2, me_col % 2
    span = NY * rows
    users = prev_in.shape[0]
    cols = 2 * NZ
    own = users // cols

    def at_row(dx, dy):
        return ((my_x + dx + NX) % NX) * NY + (my_y + dy + NY) % NY

    def base_row(row):
        return pl.multiple_of(row * rows, rows)

    peers = []
    for dz in sorted(range(NZ), key=lambda d: -min(d, NZ - d)):
        for flip in (0, 1):
            if dz or flip:
                peers.append(((my_z + dz) % NZ) * 2 + (my_core + flip) % 2)

    mine = base_row(me_row)
    loads = []
    for h in range(2):
        loads.append(
            pltpu.make_async_copy(
                item_hbm.at[:, :, pl.ds(h * HALF, HALF)],
                buf.at[pl.ds(h * TILES_COL, TILES_COL), pl.ds(mine, rows), :],
                load_sem.at[h],
            )
        )
        loads[-1].start()

    barrier = pltpu.get_barrier_semaphore()
    near = [at_row(1, 0), at_row(-1, 0), at_row(0, 1), at_row(0, -1)]
    for row in near:
        pl.semaphore_signal(barrier, inc=1, device_id=(row, me_col), device_id_type=MESH)
    for col in peers:
        pl.semaphore_signal(barrier, inc=1, device_id=(me_row, col), device_id_type=MESH)
    pl.semaphore_wait(barrier, len(near) + len(peers))
    for load in loads:
        load.wait()

    copies = {}

    def copy_of(piece):
        if piece not in copies:
            kind, axis, sign, hops, dx, dy, lo, hi = piece
            units = pl.ds(0, A_UNITS) if kind == "A" else pl.ds(A_UNITS, UNITS - A_UNITS)
            source = base_row(at_row(-dx, -dy))
            place = buf.at[units, pl.ds(source + lo, hi - lo), :]
            target = at_row(sign, 0) if axis == "x" else at_row(0, sign)
            index = len(copies)
            copies[piece] = pltpu.make_async_remote_copy(
                src_ref=place,
                dst_ref=place,
                send_sem=send_sem.at[index],
                recv_sem=recv_sem.at[index],
                device_id=(target, me_col),
                device_id_type=MESH,
            )
        return copies[piece]

    def expand():
        eye = lax.broadcasted_iota(jnp.int32, (users, users), 0) == lax.broadcasted_iota(
            jnp.int32, (users, users), 1
        )
        conf = jnp.sum(jnp.where(eye, conf_in[...], 0.0), axis=1, keepdims=True)
        words_wide = words_in.shape[1]
        lanes = 8 * words_wide
        word_of = lax.broadcasted_iota(jnp.int32, (words_wide, lanes), 0)
        slot_of = lax.broadcasted_iota(jnp.int32, (words_wide, lanes), 1)
        scale = 1.0 / jnp.left_shift(1, slot_of & 7).astype(jnp.float32)
        spreader = jnp.where((slot_of >> 3) == word_of, scale, 0.0).astype(jnp.bfloat16)
        for s in range(OBS):
            count = counts[observed[0, s]]
            for half in range(words_in.shape[0] // (users * OBS)):
                words = words_in[pl.ds(half * OBS + s, users, stride=words_in.shape[0] // users), :]
                shifted = jnp.dot(
                    words.astype(jnp.float32).astype(jnp.bfloat16),
                    spreader,
                    preferred_element_type=jnp.float32,
                ).astype(jnp.int32)
                slot = half * lanes + lax.broadcasted_iota(jnp.int32, (users, lanes), 1)
                on = jnp.where(slot < count, shifted & 1, 0).astype(jnp.float32)
                for piece in range(lanes // span):
                    chunk = half * (lanes // span) + piece
                    here = on[:, piece * span : (piece + 1) * span]
                    seen[s, chunk] = here.astype(jnp.bfloat16)
                    cs[s, chunk] = conf * here
        return conf

    def rows_of(tile, chunk):
        place = pl.ds(pl.multiple_of(chunk * span, span), span)
        return jnp.concatenate([buf[tile, place, :], buf[TILES_COL + tile, place, :]], axis=1)

    def weighted(rounded, s, chunk):
        items = picked[s, chunk]
        scores = lax.dot_general(
            rounded, items, (((1,), (1,)), ((), ())), preferred_element_type=jnp.float32
        )
        weights = (cs[s, chunk] * scores).astype(jnp.bfloat16)
        return jnp.dot(weights, items, preferred_element_type=jnp.float32)

    for piece in events[0][1]:
        copy_of(piece).start()
    start = prev_in[...].astype(jnp.float32)
    vectors[0] = start
    gram[...] = jnp.zeros_like(gram)
    part[0] = jnp.zeros_like(start)
    conf = expand()

    def first_pass(chunk):
        slot = chunk * span + lax.broadcasted_iota(jnp.int32, (span, R), 0)
        choice = [None] * OBS
        total = gram[...]
        for tile in range(TILES_COL):
            items = rows_of(tile, chunk)
            for s in range(OBS):
                choice[s] = (
                    items if tile == 0 else jnp.where(observed[0, s] == tile, items, choice[s])
                )
            valid = jnp.where(slot < counts[tile], 1.0, 0.0).astype(jnp.bfloat16)
            total = total + lax.dot_general(
                valid * items, items, (((0,), (0,)), ((), ())), preferred_element_type=jnp.float32
            )
        gram[...] = total
        sums = part[0]
        for s in range(OBS):
            picked[s, chunk] = choice[s]
            sums = sums + (1.0 + conf) * jnp.dot(
                seen[s, chunk], choice[s], preferred_element_type=jnp.float32
            )
            sums = sums - weighted(prev_in[...], s, chunk)
        part[0] = sums

    for piece, follow, _ in events[1:]:
        copy_of(piece).wait_recv()
        for other in follow:
            copy_of(other).start()

    for dx in (0, 1, 3, 2):
        first_pass((my_x + dx) % NX)

    mine_users = pl.ds(pl.multiple_of(me_col * own, own), own)
    waits = []

    def with_gram(vector):
        return jnp.dot(vector, gram[...], precision=lax.Precision.HIGHEST)

    def exchange_sums(k):
        for col in peers:
            copy = pltpu.make_async_remote_copy(
                src_ref=part.at[k, pl.ds(pl.multiple_of(col * own, own), own), :],
                dst_ref=heard.at[k, me_col],
                send_sem=sum_send.at[k],
                recv_sem=sum_recv.at[k],
                device_id=(me_row, col),
                device_id_type=MESH,
            )
            copy.start()
        heard[k, me_col] = part[k, mine_users, :]
        several = heard.at[k, pl.ds(0, cols - 1)]
        pltpu.make_async_copy(several, several, sum_recv.at[k]).wait()
        waits.append((several, sum_send.at[k]))
        total = heard[k, 0]
        for col in range(1, cols):
            total = total + heard[k, col]
        return total

    def share(k, value):
        vectors[k, mine_users, :] = value
        for col in peers:
            copy = pltpu.make_async_remote_copy(
                src_ref=vectors.at[k, mine_users, :],
                dst_ref=vectors.at[k, mine_users, :],
                send_sem=vec_send.at[k],
                recv_sem=vec_recv.at[k],
                device_id=(me_row, col),
                device_id_type=MESH,
            )
            copy.start()
        several = vectors.at[k, pl.ds(0, own * (cols - 1)), :]
        pltpu.make_async_copy(several, several, vec_recv.at[k]).wait()
        waits.append((several, vec_send.at[k]))

    part[0] = part[0] - with_gram(start)
    answer = vectors[0, mine_users, :]
    residual = exchange_sums(0) - RIDGE * answer
    direction = residual
    norm_now = jnp.sum(residual * residual, axis=1, keepdims=True)
    for k in range(1, ITERS + 1):
        share(k, direction)
        vector = vectors[k]
        rounded = vector.astype(jnp.bfloat16)
        sums = with_gram(vector)
        for s in range(OBS):
            for chunk in range(NX):
                sums = sums + weighted(rounded, s, chunk)
        part[k] = sums
        image = exchange_sums(k) + RIDGE * direction
        step_size = norm_now / jnp.sum(direction * image, axis=1, keepdims=True)
        answer = answer + step_size * direction
        if k < ITERS:
            residual = residual - step_size * image
            norm_next = jnp.sum(residual * residual, axis=1, keepdims=True)
            direction = residual + (norm_next / norm_now) * direction
            norm_now = norm_next
    share(ITERS + 1, answer)
    out_ref[...] = vectors[ITERS + 1]

    for piece in copies:
        copies[piece].wait_send()
    for several, sem in waits:
        pltpu.make_async_copy(several, several, sem).wait()


def local(item_factors, tile_counts, observed_tiles, mask_words, confidence, previous):
    rows = item_factors.shape[1]
    users, slots, words = mask_words.shape
    tile_len = NX * NY * rows
    events = plan(rows)
    messages = sum(len(follow) for _, follow, _ in events)
    flat = (
        mask_words.reshape(users, slots, words // HALF, HALF)
        .transpose(0, 2, 1, 3)
        .reshape(users * slots * (words // HALF), HALF)
    )
    vmem = pl.BlockSpec(memory_space=pltpu.VMEM)
    smem = pl.BlockSpec(memory_space=pltpu.SMEM)
    cols = 2 * NZ
    return pl.pallas_call(
        functools.partial(kernel, events=events, rows=rows),
        out_shape=jax.ShapeDtypeStruct((users, R), jnp.float32),
        in_specs=[smem, smem, vmem, vmem, vmem, pl.BlockSpec(memory_space=pl.ANY)],
        out_specs=vmem,
        scratch_shapes=[
            pltpu.VMEM((UNITS, tile_len, HALF), jnp.bfloat16),
            pltpu.VMEM((OBS, NX, NY * rows, R), jnp.bfloat16),
            pltpu.VMEM((OBS, NX, users, NY * rows), jnp.float32),
            pltpu.VMEM((OBS, NX, users, NY * rows), jnp.bfloat16),
            pltpu.VMEM((ITERS + 1, users, R), jnp.float32),
            pltpu.VMEM((ITERS + 1, cols, users // cols, R), jnp.float32),
            pltpu.VMEM((ITERS + 2, users, R), jnp.float32),
            pltpu.VMEM((R, R), jnp.float32),
            pltpu.SemaphoreType.DMA((2,)),
            pltpu.SemaphoreType.DMA((messages,)),
            pltpu.SemaphoreType.DMA((messages,)),
            pltpu.SemaphoreType.DMA((ITERS + 1,)),
            pltpu.SemaphoreType.DMA((ITERS + 1,)),
            pltpu.SemaphoreType.DMA((ITERS + 2,)),
            pltpu.SemaphoreType.DMA((ITERS + 2,)),
        ],
        compiler_params=pltpu.CompilerParams(
            collective_id=0, has_side_effects=True, vmem_limit_bytes=48 * 2**20
        ),
    )(tile_counts, observed_tiles, confidence.reshape(1, users), previous, flat, item_factors)


def solution(mesh):
    return jax.shard_map(
        local,
        mesh=mesh,
        in_specs=(
            P("col", "row", None),
            P("col"),
            P("row", "col"),
            P("row", "col", None),
            P("row"),
            P("row", None),
        ),
        out_specs=P("row", None),
        check_vma=False,
    )
```

```python
import functools
import heapq
import itertools

import jax
import jax.numpy as jnp
from jax import lax
from jax.experimental import pallas as pl
from jax.experimental.pallas import tpu as pltpu
from jax.sharding import PartitionSpec as P

R = 256
HALF = 128
OBS = 2
ITERS = 3
TILES_COL = 4
UNITS = 2 * TILES_COL
RIDGE = 0.1
NX, NY, NZ = 4, 8, 8
A_UNITS = 5
MESH = pl.DeviceIdType.MESH


def plan(rows):
    a_us, b_us = 1.76 * A_UNITS / 5, 1.76 * (UNITS - A_UNITS) / 5
    free = {}
    heap = []
    order = []
    ready = []
    events = []
    tick = itertools.count()

    def queue(*piece):
        kind, axis, _, hops = piece[:4]
        if kind == "A":
            left = 6 - hops if axis == "y" else 2 - hops
        else:
            left = 6 - hops if axis == "x" else 4 - hops
        ready.append((-left, next(tick), piece))

    def flush(now):
        for _, _, piece in sorted(ready):
            kind, axis, sign, lo, hi, stride = piece[0], piece[1], piece[2], *piece[6:]
            cost = (a_us if kind == "A" else b_us) * (hi - lo) / rows
            begin = max(now, free.get((axis, sign), 0.0))
            free[axis, sign] = begin + cost * stride
            heapq.heappush(heap, (begin + cost + 2.5 + 0.5 * stride, next(tick), piece))
            order.append(piece)
        ready.clear()
        events.append((heard[0], list(order), now))
        order.clear()

    def spread(kind, axis, dx, dy, lo, hi):
        for stride in (2, 1) if (kind, axis) == ("A", "y") else (1,):
            for sign in (1, -1):
                queue(kind, axis, sign, stride, dx, dy, lo, hi, stride)

    heard = [None]
    spread("A", "y", 0, 0, 0, rows)
    spread("B", "x", 0, 0, 0, rows)
    spread("A", "x", 0, 0, 0, rows)
    spread("B", "y", 0, 0, 0, rows)
    flush(0.0)
    while heap:
        now, _, heard[0] = heapq.heappop(heap)
        kind, axis, sign, hops, dx, dy, lo, hi, stride = heard[0]
        last = (NX if axis == "x" else NY) // 2
        if axis == "x":
            dx += sign * stride
        else:
            dy += sign * stride
        if hops < last and not (kind == "A" and axis == "y" and hops == 1):
            middle = (lo + hi) // 2
            if hops < last - 1:
                queue(kind, axis, sign, hops + 1, dx, dy, lo, hi, 1)
            elif sign == 1:
                queue(kind, axis, sign, hops + 1, dx, dy, lo, middle, 1)
            else:
                queue(kind, axis, sign, hops + 1, dx, dy, middle, hi, 1)
        if (kind, axis) == ("A", "y"):
            spread("A", "x", dx, dy, lo, hi)
        if (kind, axis) == ("B", "x"):
            spread("B", "y", dx, dy, lo, hi)
        flush(now)
    return events


def kernel(
    counts_hbm,
    observed_hbm,
    conf_hbm,
    prev_hbm,
    words_hbm,
    item_hbm,
    out_ref,
    buf,
    picked,
    cs,
    seen,
    part,
    heard,
    high,
    low,
    steps,
    dots,
    gram,
    counts,
    observed,
    conf_in,
    prev_in,
    words_in,
    load_sem,
    send_sem,
    recv_sem,
    sum_send,
    sum_recv,
    high_send,
    high_recv,
    low_send,
    low_recv,
    step_sem,
    dot_sem,
    *,
    events,
    rows,
):
    me_row = lax.axis_index("row")
    me_col = lax.axis_index("col")
    my_x, my_y = me_row // NY, me_row % NY
    my_z, my_core = me_col // 2, me_col % 2
    span = NY * rows
    users = prev_in.shape[0]
    cols = 2 * NZ
    own = users // cols

    def at_row(dx, dy):
        return ((my_x + dx + NX) % NX) * NY + (my_y + dy + NY) % NY

    def base_row(row):
        return pl.multiple_of(row * rows, rows)

    peers = []
    for dz in sorted(range(NZ), key=lambda d: -min(d, NZ - d)):
        for flip in (0, 1):
            if dz or flip:
                peers.append(((my_z + dz) % NZ) * 2 + (my_core + flip) % 2)

    mine = base_row(me_row)
    loads = []
    for h in range(2):
        loads.append(
            pltpu.make_async_copy(
                item_hbm.at[:, :, pl.ds(h * HALF, HALF)],
                buf.at[pl.ds(h * TILES_COL, TILES_COL), pl.ds(mine, rows), :],
                load_sem.at[h],
            )
        )
        loads[-1].start()
    others = []
    for i, (src, dst) in enumerate(
        (
            (words_hbm, words_in),
            (counts_hbm, counts),
            (observed_hbm, observed),
            (conf_hbm, conf_in),
            (prev_hbm, prev_in),
        )
    ):
        others.append(pltpu.make_async_copy(src, dst, load_sem.at[2 + i]))
        others[-1].start()

    barrier = pltpu.get_barrier_semaphore()
    near = [at_row(1, 0), at_row(-1, 0)] + [at_row(0, d) for d in (1, -1, 2, -2)]
    for row in near:
        pl.semaphore_signal(barrier, inc=1, device_id=(row, me_col), device_id_type=MESH)
    for col in peers:
        pl.semaphore_signal(barrier, inc=1, device_id=(me_row, col), device_id_type=MESH)
    pl.semaphore_wait(barrier, len(near) + len(peers))
    for load in loads:
        load.wait()

    copies = {}

    def copy_of(piece):
        if piece not in copies:
            kind, axis, sign, _, dx, dy, lo, hi, stride = piece
            units = pl.ds(0, A_UNITS) if kind == "A" else pl.ds(A_UNITS, UNITS - A_UNITS)
            source = base_row(at_row(-dx, -dy))
            place = buf.at[units, pl.ds(source + lo, hi - lo), :]
            target = at_row(sign, 0) if axis == "x" else at_row(0, sign * stride)
            index = len(copies)
            copies[piece] = pltpu.make_async_remote_copy(
                src_ref=place,
                dst_ref=place,
                send_sem=send_sem.at[index],
                recv_sem=recv_sem.at[index],
                device_id=(target, me_col),
                device_id_type=MESH,
            )
        return copies[piece]

    eye = lax.broadcasted_iota(jnp.int32, (users, users), 0) == lax.broadcasted_iota(
        jnp.int32, (users, users), 1
    )

    def column(row):
        return jnp.sum(jnp.where(eye, row, 0.0), axis=1, keepdims=True)

    def expand():
        conf = column(conf_in[...])
        words_wide = words_in.shape[1]
        lanes = 8 * words_wide
        word_of = lax.broadcasted_iota(jnp.int32, (words_wide, lanes), 0)
        slot_of = lax.broadcasted_iota(jnp.int32, (words_wide, lanes), 1)
        scale = 1.0 / jnp.left_shift(1, slot_of & 7).astype(jnp.float32)
        spreader = jnp.where((slot_of >> 3) == word_of, scale, 0.0).astype(jnp.bfloat16)
        for s in range(OBS):
            count = counts[observed[0, s]]
            for half in range(words_in.shape[0] // (users * OBS)):
                words = words_in[pl.ds(half * OBS + s, users, stride=words_in.shape[0] // users), :]
                shifted = jnp.dot(
                    words.astype(jnp.float32).astype(jnp.bfloat16),
                    spreader,
                    preferred_element_type=jnp.float32,
                ).astype(jnp.int32)
                slot = half * lanes + lax.broadcasted_iota(jnp.int32, (users, lanes), 1)
                on = jnp.where(slot < count, shifted & 1, 0).astype(jnp.float32)
                for piece in range(lanes // span):
                    chunk = half * (lanes // span) + piece
                    here = on[:, piece * span : (piece + 1) * span]
                    seen[s, chunk] = here.astype(jnp.bfloat16)
                    cs[s, chunk] = conf * here
        return conf

    def rows_of(tile, chunk):
        place = pl.ds(pl.multiple_of(chunk * span, span), span)
        return jnp.concatenate([buf[tile, place, :], buf[TILES_COL + tile, place, :]], axis=1)

    def weighted(rounded, s, chunk):
        items = picked[s, chunk]
        scores = lax.dot_general(
            rounded, items, (((1,), (1,)), ((), ())), preferred_element_type=jnp.float32
        )
        weights = (cs[s, chunk] * scores).astype(jnp.bfloat16)
        return jnp.dot(weights, items, preferred_element_type=jnp.float32)

    for piece in events[0][1]:
        copy_of(piece).start()
    for load in others:
        load.wait()
    gram[...] = jnp.zeros_like(gram)
    part[0] = jnp.zeros((users, R), jnp.float32)
    conf = expand()

    def first_pass(chunk):
        slot = chunk * span + lax.broadcasted_iota(jnp.int32, (span, R), 0)
        choice = [None] * OBS
        total = gram[...]
        for tile in range(TILES_COL):
            items = rows_of(tile, chunk)
            for s in range(OBS):
                choice[s] = (
                    items if tile == 0 else jnp.where(observed[0, s] == tile, items, choice[s])
                )
            valid = jnp.where(slot < counts[tile], 1.0, 0.0).astype(jnp.bfloat16)
            total = total + lax.dot_general(
                valid * items, items, (((0,), (0,)), ((), ())), preferred_element_type=jnp.float32
            )
        gram[...] = total
        sums = part[0]
        for s in range(OBS):
            picked[s, chunk] = choice[s]
            sums = sums + (1.0 + conf) * jnp.dot(
                seen[s, chunk], choice[s], preferred_element_type=jnp.float32
            )
            sums = sums - weighted(prev_in[...], s, chunk)
        part[0] = sums

    done = {}
    for index, (piece, _, _) in enumerate(events[1:]):
        _, axis, sign, _, dx, _, _, _, stride = piece
        done[(-dx - (sign * stride if axis == "x" else 0)) % NX] = index
    for index, (piece, follow, _) in enumerate(events[1:]):
        copy_of(piece).wait_recv()
        for other in follow:
            copy_of(other).start()
        for dx in range(NX):
            if done[dx] == index:
                first_pass((my_x + dx) % NX)

    waits = []

    def finish(ref, sem):
        pltpu.make_async_copy(ref, ref, sem).wait()

    def to_peers(place, send, recv):
        for col in peers:
            pltpu.make_async_remote_copy(
                src_ref=place.at[me_col],
                dst_ref=place.at[me_col],
                send_sem=send,
                recv_sem=recv,
                device_id=(me_row, col),
                device_id_type=MESH,
            ).start()
        waits.append((place.at[pl.ds(0, cols - 1)], send))

    def with_gram(vector):
        return jnp.dot(
            vector,
            gram[...],
            precision=lax.Precision.HIGHEST,
            preferred_element_type=jnp.float32,
        )

    def exchange_sums(k):
        for col in peers:
            pltpu.make_async_remote_copy(
                src_ref=part.at[k, pl.ds(pl.multiple_of(col * own, own), own), :],
                dst_ref=heard.at[k, me_col],
                send_sem=sum_send.at[k],
                recv_sem=sum_recv.at[k],
                device_id=(me_row, col),
                device_id_type=MESH,
            ).start()
        heard[k, me_col] = part[k, pl.ds(pl.multiple_of(me_col * own, own), own), :]
        several = heard.at[k, pl.ds(0, cols - 1)]
        waits.append((several, sum_send.at[k]))
        finish(several, sum_recv.at[k])
        total = heard[k, 0]
        for col in range(1, cols):
            total = total + heard[k, col]
        return total

    def whole(ref, k):
        return ref[k].astype(jnp.float32).reshape(users, R)

    start = prev_in[...].astype(jnp.float32)
    part[0] = part[0] - with_gram(start)
    mine_users = (
        lax.broadcasted_iota(jnp.int32, (own, users), 1)
        == me_col * own + lax.broadcasted_iota(jnp.int32, (own, users), 0)
    ).astype(jnp.float32).astype(jnp.bfloat16)
    ours = jnp.dot(mine_users, prev_in[...], preferred_element_type=jnp.float32)
    residual = exchange_sums(0) - RIDGE * ours
    direction = residual
    norm_now = jnp.sum(residual * residual, axis=1, keepdims=True)
    lane = lax.broadcasted_iota(jnp.int32, (own, HALF), 1)
    scalars = jnp.zeros((own, HALF), jnp.float32)
    for k in range(ITERS):
        top = direction.astype(jnp.bfloat16)
        rest = (direction - top.astype(jnp.float32)).astype(jnp.bfloat16)
        high[k, me_col] = top
        low[k, me_col] = rest
        to_peers(high.at[k], high_send.at[k], high_recv.at[k])
        to_peers(low.at[k], low_send.at[k], low_recv.at[k])
        if k == ITERS - 1:
            steps[me_col] = jnp.where(lane == k, norm_now, scalars)
            to_peers(steps, step_sem.at[0], step_sem.at[1])
        direction = top.astype(jnp.float32) + rest.astype(jnp.float32)
        finish(high.at[k, pl.ds(0, cols - 1)], high_recv.at[k])
        upper = whole(high, k)
        rounded = upper.astype(jnp.bfloat16)
        sums = jnp.zeros((users, R), jnp.float32)
        for s in range(OBS):
            for chunk in range(NX):
                sums = sums + weighted(rounded, s, chunk)
        finish(low.at[k, pl.ds(0, cols - 1)], low_recv.at[k])
        vector = upper + whole(low, k)
        sums = sums + with_gram(vector)
        if k == ITERS - 1:
            break
        part[k + 1] = sums
        image = exchange_sums(k + 1) + RIDGE * direction
        step_size = norm_now / jnp.sum(direction * image, axis=1, keepdims=True)
        scalars = jnp.where(lane == k, step_size, scalars)
        residual = residual - step_size * image
        norm_next = jnp.sum(residual * residual, axis=1, keepdims=True)
        direction = residual + (norm_next / norm_now) * direction
        norm_now = norm_next

    dot_here = jnp.sum(sums * vector, axis=1, keepdims=True)
    dots[me_col] = jnp.broadcast_to(
        jnp.sum(jnp.where(eye, dot_here, 0.0), axis=0, keepdims=True), (8, users)
    )
    to_peers(dots, dot_sem.at[0], dot_sem.at[1])
    finish(steps.at[pl.ds(0, cols - 1)], step_sem.at[1])
    known = steps[...].reshape(users, HALF)
    answer = start
    for k in range(ITERS - 1):
        answer = answer + known[:, k : k + 1] * (whole(high, k) + whole(low, k))
    ridge = RIDGE * jnp.sum(vector * vector, axis=1, keepdims=True)
    finish(dots.at[pl.ds(0, cols - 1)], dot_sem.at[1])
    total = dots[0, 0:1]
    for col in range(1, cols):
        total = total + dots[col, 0:1]
    step_size = known[:, ITERS - 1 : ITERS] / (column(total) + ridge)
    out_ref[...] = answer + step_size * vector

    for piece in copies:
        copies[piece].wait_send()
    for several, sem in waits:
        finish(several, sem)


def local(item_factors, tile_counts, observed_tiles, mask_words, confidence, previous):
    rows = item_factors.shape[1]
    users, slots, words = mask_words.shape
    tile_len = NX * NY * rows
    events = plan(rows)
    messages = sum(len(follow) for _, follow, _ in events)
    flat = (
        mask_words.reshape(users, slots, words // HALF, HALF)
        .transpose(0, 2, 1, 3)
        .reshape(users * slots * (words // HALF), HALF)
    )
    anywhere = pl.BlockSpec(memory_space=pl.ANY)
    cols = 2 * NZ
    own = users // cols
    sems = pltpu.SemaphoreType.DMA
    return pl.pallas_call(
        functools.partial(kernel, events=events, rows=rows),
        out_shape=jax.ShapeDtypeStruct((users, R), jnp.float32),
        in_specs=[anywhere] * 6,
        out_specs=pl.BlockSpec(memory_space=pltpu.VMEM),
        scratch_shapes=[
            pltpu.VMEM((UNITS, tile_len, HALF), jnp.bfloat16),
            pltpu.VMEM((OBS, NX, NY * rows, R), jnp.bfloat16),
            pltpu.VMEM((OBS, NX, users, NY * rows), jnp.float32),
            pltpu.VMEM((OBS, NX, users, NY * rows), jnp.bfloat16),
            pltpu.VMEM((ITERS, users, R), jnp.float32),
            pltpu.VMEM((ITERS, cols, own, R), jnp.float32),
            pltpu.VMEM((ITERS, cols, own, R), jnp.bfloat16),
            pltpu.VMEM((ITERS, cols, own, R), jnp.bfloat16),
            pltpu.VMEM((cols, own, HALF), jnp.float32),
            pltpu.VMEM((cols, 8, users), jnp.float32),
            pltpu.VMEM((R, R), jnp.float32),
            pltpu.SMEM(tile_counts.shape, jnp.int32),
            pltpu.SMEM(observed_tiles.shape, jnp.int32),
            pltpu.VMEM((1, users), jnp.float32),
            pltpu.VMEM((users, R), jnp.bfloat16),
            pltpu.VMEM(flat.shape, jnp.int32),
            sems((7,)),
            sems((messages,)),
            sems((messages,)),
        ]
        + [sems((ITERS,))] * 6
        + [sems((2,))] * 2,
        compiler_params=pltpu.CompilerParams(
            collective_id=0, has_side_effects=True, vmem_limit_bytes=60 * 1024 * 1024
        ),
    )(tile_counts, observed_tiles, confidence.reshape(1, users), previous, flat, item_factors)


def solution(mesh):
    return jax.shard_map(
        local,
        mesh=mesh,
        in_specs=(
            P("col", "row", None),
            P("col"),
            P("row", "col"),
            P("row", "col", None),
            P("row"),
            P("row", None),
        ),
        out_specs=P("row", None),
        check_vma=False,
    )
```

```python
import functools
import heapq
import itertools

import jax
import jax.numpy as jnp
from jax import lax
from jax.experimental import pallas as pl
from jax.experimental.pallas import tpu as pltpu
from jax.sharding import PartitionSpec as P

R = 256
HALF = 128
OBS = 2
ITERS = 3
TILES_COL = 4
UNITS = 2 * TILES_COL
RIDGE = 0.1
NX, NY, NZ = 4, 8, 8
A_UNITS = 5
MESH = pl.DeviceIdType.MESH


SPLIT = 1


def plan(rows):
    unit_us = 1.76 / 5
    costs = {"A": unit_us * A_UNITS, "B": unit_us * (UNITS - A_UNITS)}
    free = {(axis, sign): 0.0 for axis in "xy" for sign in (1, -1)}
    waiting = {link: [] for link in free}
    heap = []
    events = []
    tick = itertools.count()

    def queue(*piece):
        kind, axis, sign, hops, dx, dy = piece[:6]
        turn = -(6 - hops if (kind, axis) in (("A", "y"), ("B", "x")) else (2 if kind == "A" else 4) - hops)
        heapq.heappush(waiting[axis, sign], (turn, next(tick), piece))

    def flush(now, heard):
        order = []
        for link, line in waiting.items():
            while line:
                piece = heapq.heappop(line)[2]
                lo, hi, stride = piece[6:]
                cost = costs[piece[0]] * (hi - lo) / rows
                begin = max(now, free[link])
                free[link] = begin + cost * stride
                heapq.heappush(heap, (begin + cost + 2.5 + 0.5 * stride, next(tick), piece))
                order.append(piece)
        events.append((heard, order, now))

    def spread(kind, axis, dx, dy, lo, hi):
        for stride in (2, 1) if (kind, axis) == ("A", "y") else (1,):
            for sign in (1, -1):
                queue(kind, axis, sign, stride, dx, dy, lo, hi, stride)

    for part in range(SPLIT):
        lo, hi = rows * part // SPLIT, rows * (part + 1) // SPLIT
        for kind, axis in (("A", "y"), ("B", "x"), ("A", "x"), ("B", "y")):
            spread(kind, axis, 0, 0, lo, hi)
    flush(0.0, None)
    while heap:
        now, _, heard = heapq.heappop(heap)
        kind, axis, sign, hops, dx, dy, lo, hi, stride = heard
        last = (NX if axis == "x" else NY) // 2
        if axis == "x":
            dx += sign * stride
        else:
            dy += sign * stride
        if hops < last and not (kind == "A" and axis == "y" and hops == 1):
            middle = (lo + hi) // 2
            if hops < last - 1:
                queue(kind, axis, sign, hops + 1, dx, dy, lo, hi, 1)
            elif sign == 1:
                queue(kind, axis, sign, hops + 1, dx, dy, lo, middle, 1)
            else:
                queue(kind, axis, sign, hops + 1, dx, dy, middle, hi, 1)
        if (kind, axis) == ("A", "y"):
            spread("A", "x", dx, dy, lo, hi)
        if (kind, axis) == ("B", "x"):
            spread("B", "y", dx, dy, lo, hi)
        flush(now, heard)
    return events


def kernel(
    counts_hbm,
    observed_hbm,
    conf_hbm,
    prev_hbm,
    words_hbm,
    item_hbm,
    out_ref,
    buf,
    picked,
    turned,
    cs,
    seen,
    part,
    heard,
    high,
    low,
    steps,
    dots,
    gram,
    counts,
    observed,
    conf_in,
    prev_in,
    words_in,
    load_sem,
    send_sem,
    recv_sem,
    sum_send,
    sum_recv,
    high_send,
    high_recv,
    low_send,
    low_recv,
    step_sem,
    dot_sem,
    *,
    events,
    rows,
):
    me_row = lax.axis_index("row")
    me_col = lax.axis_index("col")
    my_x, my_y = me_row // NY, me_row % NY
    my_z, my_core = me_col // 2, me_col % 2
    span = NY * rows
    users = prev_in.shape[0]
    cols = 2 * NZ
    own = users // cols

    def at_row(dx, dy):
        return ((my_x + dx + NX) % NX) * NY + (my_y + dy + NY) % NY

    def base_row(row):
        return pl.multiple_of(row * rows, rows)

    peers = []
    for dz in sorted(range(NZ), key=lambda d: -min(d, NZ - d)):
        for flip in (0, 1):
            if dz or flip:
                peers.append(((my_z + dz) % NZ) * 2 + (my_core + flip) % 2)

    mine = base_row(me_row)
    barrier = pltpu.get_barrier_semaphore()
    near = [at_row(1, 0), at_row(-1, 0)] + [at_row(0, d) for d in (1, -1, 2, -2)]
    for row in near:
        pl.semaphore_signal(barrier, inc=1, device_id=(row, me_col), device_id_type=MESH)
    for col in peers:
        pl.semaphore_signal(barrier, inc=1, device_id=(me_row, col), device_id_type=MESH)
    loads = []
    for h in range(2):
        loads.append(
            pltpu.make_async_copy(
                item_hbm.at[:, :, pl.ds(h * HALF, HALF)],
                buf.at[pl.ds(h * TILES_COL, TILES_COL), pl.ds(mine, rows), :],
                load_sem.at[h],
            )
        )
        loads[-1].start()
    others = []
    for i, (src, dst) in enumerate(
        (
            (words_hbm, words_in),
            (counts_hbm, counts),
            (observed_hbm, observed),
            (conf_hbm, conf_in),
            (prev_hbm, prev_in),
        )
    ):
        others.append(pltpu.make_async_copy(src, dst, load_sem.at[2 + i]))
        others[-1].start()

    pl.semaphore_wait(barrier, len(near) + len(peers))
    for load in loads:
        load.wait()

    copies = {}

    def copy_of(piece):
        if piece not in copies:
            kind, axis, sign, _, dx, dy, lo, hi, stride = piece
            units = pl.ds(0, A_UNITS) if kind == "A" else pl.ds(A_UNITS, UNITS - A_UNITS)
            source = base_row(at_row(-dx, -dy))
            place = buf.at[units, pl.ds(source + lo, hi - lo), :]
            target = at_row(sign, 0) if axis == "x" else at_row(0, sign * stride)
            index = len(copies)
            copies[piece] = pltpu.make_async_remote_copy(
                src_ref=place,
                dst_ref=place,
                send_sem=send_sem.at[index],
                recv_sem=recv_sem.at[index],
                device_id=(target, me_col),
                device_id_type=MESH,
            )
        return copies[piece]

    eye = lax.broadcasted_iota(jnp.int32, (users, users), 0) == lax.broadcasted_iota(
        jnp.int32, (users, users), 1
    )

    def column(row):
        return jnp.sum(jnp.where(eye, row, 0.0), axis=1, keepdims=True)

    def expand():
        conf = column(conf_in[...])
        words_wide = words_in.shape[1]
        lanes = 8 * words_wide
        word_of = lax.broadcasted_iota(jnp.int32, (words_wide, lanes), 0)
        slot_of = lax.broadcasted_iota(jnp.int32, (words_wide, lanes), 1)
        scale = 1.0 / jnp.left_shift(1, slot_of & 7).astype(jnp.float32)
        spreader = jnp.where((slot_of >> 3) == word_of, scale, 0.0).astype(jnp.bfloat16)
        for s in range(OBS):
            count = counts[observed[0, s]]
            for half in range(words_in.shape[0] // (users * OBS)):
                words = words_in[pl.ds(half * OBS + s, users, stride=words_in.shape[0] // users), :]
                shifted = jnp.dot(
                    words.astype(jnp.float32).astype(jnp.bfloat16),
                    spreader,
                    preferred_element_type=jnp.float32,
                ).astype(jnp.int32)
                slot = half * lanes + lax.broadcasted_iota(jnp.int32, (users, lanes), 1)
                on = jnp.where(slot < count, shifted & 1, 0).astype(jnp.float32)
                for piece in range(lanes // span):
                    chunk = half * (lanes // span) + piece
                    here = on[:, piece * span : (piece + 1) * span]
                    seen[s, chunk] = here.astype(jnp.bfloat16)
                    cs[s, chunk] = conf * here
        return conf

    def rows_of(tile, chunk):
        place = pl.ds(pl.multiple_of(chunk * span, span), span)
        return jnp.concatenate([buf[tile, place, :], buf[TILES_COL + tile, place, :]], axis=1)

    def weighted(rounded, s, chunk):
        scores = jnp.dot(rounded, turned[s, chunk], preferred_element_type=jnp.float32)
        weights = (cs[s, chunk] * scores).astype(jnp.bfloat16)
        return jnp.dot(weights, picked[s, chunk], preferred_element_type=jnp.float32)

    for piece in events[0][1]:
        copy_of(piece).start()
    for load in others:
        load.wait()
    gram[...] = jnp.zeros_like(gram)
    part[0] = jnp.zeros((users, R), jnp.float32)
    conf = expand()

    def first_pass(chunk):
        slot = chunk * span + lax.broadcasted_iota(jnp.int32, (span, R), 0)
        choice = [None] * OBS
        total = gram[...]
        for tile in range(TILES_COL):
            items = rows_of(tile, chunk)
            for s in range(OBS):
                choice[s] = (
                    items if tile == 0 else jnp.where(observed[0, s] == tile, items, choice[s])
                )
            valid = jnp.where(slot < counts[tile], 1.0, 0.0).astype(jnp.bfloat16)
            total = total + lax.dot_general(
                valid * items, items, (((0,), (0,)), ((), ())), preferred_element_type=jnp.float32
            )
        gram[...] = total
        sums = part[0]
        for s in range(OBS):
            picked[s, chunk] = choice[s]
            turned[s, chunk] = choice[s].T
            sums = sums + (1.0 + conf) * jnp.dot(
                seen[s, chunk], choice[s], preferred_element_type=jnp.float32
            )
            sums = sums - weighted(prev_in[...], s, chunk)
        part[0] = sums

    done = {}
    for index, (piece, _, _) in enumerate(events[1:]):
        _, axis, sign, _, dx, _, _, _, stride = piece
        done[(-dx - (sign * stride if axis == "x" else 0)) % NX] = index
    for index, (piece, follow, _) in enumerate(events[1:]):
        copy_of(piece).wait_recv()
        for other in follow:
            copy_of(other).start()
        for dx in range(NX):
            if done[dx] == index:
                first_pass((my_x + dx) % NX)

    waits = []

    def finish(ref, sem):
        pltpu.make_async_copy(ref, ref, sem).wait()

    def to_peers(place, send, recv):
        for col in peers:
            pltpu.make_async_remote_copy(
                src_ref=place.at[me_col],
                dst_ref=place.at[me_col],
                send_sem=send,
                recv_sem=recv,
                device_id=(me_row, col),
                device_id_type=MESH,
            ).start()
        waits.append((place.at[pl.ds(0, cols - 1)], send))

    def with_gram(vector):
        return jnp.dot(
            vector,
            gram[...],
            precision=lax.Precision.HIGHEST,
            preferred_element_type=jnp.float32,
        )

    def exchange_sums(k):
        for col in peers:
            pltpu.make_async_remote_copy(
                src_ref=part.at[k, pl.ds(pl.multiple_of(col * own, own), own), :],
                dst_ref=heard.at[k, me_col],
                send_sem=sum_send.at[k],
                recv_sem=sum_recv.at[k],
                device_id=(me_row, col),
                device_id_type=MESH,
            ).start()
        heard[k, me_col] = part[k, pl.ds(pl.multiple_of(me_col * own, own), own), :]
        several = heard.at[k, pl.ds(0, cols - 1)]
        waits.append((several, sum_send.at[k]))
        finish(several, sum_recv.at[k])
        total = heard[k, 0]
        for col in range(1, cols):
            total = total + heard[k, col]
        return total

    def whole(ref, k):
        return ref[k].astype(jnp.float32).reshape(users, R)

    start = prev_in[...].astype(jnp.float32)
    part[0] = part[0] - with_gram(start)
    mine_users = (
        lax.broadcasted_iota(jnp.int32, (own, users), 1)
        == me_col * own + lax.broadcasted_iota(jnp.int32, (own, users), 0)
    ).astype(jnp.float32).astype(jnp.bfloat16)
    ours = jnp.dot(mine_users, prev_in[...], preferred_element_type=jnp.float32)
    residual = exchange_sums(0) - RIDGE * ours
    direction = residual
    norm_now = jnp.sum(residual * residual, axis=1, keepdims=True)
    lane = lax.broadcasted_iota(jnp.int32, (own, HALF), 1)
    scalars = jnp.zeros((own, HALF), jnp.float32)
    for k in range(ITERS):
        top = direction.astype(jnp.bfloat16)
        rest = (direction - top.astype(jnp.float32)).astype(jnp.bfloat16)
        high[k, me_col] = top
        low[k, me_col] = rest
        to_peers(high.at[k], high_send.at[k], high_recv.at[k])
        to_peers(low.at[k], low_send.at[k], low_recv.at[k])
        if k == ITERS - 1:
            steps[me_col] = jnp.where(lane == k, norm_now, scalars)
            to_peers(steps, step_sem.at[0], step_sem.at[1])
        direction = top.astype(jnp.float32) + rest.astype(jnp.float32)
        finish(high.at[k, pl.ds(0, cols - 1)], high_recv.at[k])
        upper = whole(high, k)
        rounded = upper.astype(jnp.bfloat16)
        sums = jnp.zeros((users, R), jnp.float32)
        for s in range(OBS):
            for chunk in range(NX):
                sums = sums + weighted(rounded, s, chunk)
        finish(low.at[k, pl.ds(0, cols - 1)], low_recv.at[k])
        vector = upper + whole(low, k)
        sums = sums + with_gram(vector)
        if k == ITERS - 1:
            break
        part[k + 1] = sums
        image = exchange_sums(k + 1) + RIDGE * direction
        step_size = norm_now / jnp.sum(direction * image, axis=1, keepdims=True)
        scalars = jnp.where(lane == k, step_size, scalars)
        residual = residual - step_size * image
        norm_next = jnp.sum(residual * residual, axis=1, keepdims=True)
        direction = residual + (norm_next / norm_now) * direction
        norm_now = norm_next

    dot_here = jnp.sum(sums * vector, axis=1, keepdims=True)
    dots[me_col] = jnp.broadcast_to(
        jnp.sum(jnp.where(eye, dot_here, 0.0), axis=0, keepdims=True), (8, users)
    )
    to_peers(dots, dot_sem.at[0], dot_sem.at[1])
    finish(steps.at[pl.ds(0, cols - 1)], step_sem.at[1])
    known = steps[...].reshape(users, HALF)
    answer = start
    for k in range(ITERS - 1):
        answer = answer + known[:, k : k + 1] * (whole(high, k) + whole(low, k))
    ridge = RIDGE * jnp.sum(vector * vector, axis=1, keepdims=True)
    finish(dots.at[pl.ds(0, cols - 1)], dot_sem.at[1])
    total = dots[0, 0:1]
    for col in range(1, cols):
        total = total + dots[col, 0:1]
    step_size = known[:, ITERS - 1 : ITERS] / (column(total) + ridge)
    out_ref[...] = answer + step_size * vector

    for piece in copies:
        copies[piece].wait_send()
    for several, sem in waits:
        finish(several, sem)


def local(item_factors, tile_counts, observed_tiles, mask_words, confidence, previous):
    rows = item_factors.shape[1]
    users, slots, words = mask_words.shape
    tile_len = NX * NY * rows
    events = plan(rows)
    messages = sum(len(follow) for _, follow, _ in events)
    flat = (
        mask_words.reshape(users, slots, words // HALF, HALF)
        .transpose(0, 2, 1, 3)
        .reshape(users * slots * (words // HALF), HALF)
    )
    anywhere = pl.BlockSpec(memory_space=pltpu.HBM)
    cols = 2 * NZ
    own = users // cols
    sems = pltpu.SemaphoreType.DMA
    return pl.pallas_call(
        functools.partial(kernel, events=events, rows=rows),
        out_shape=jax.ShapeDtypeStruct((users, R), jnp.float32),
        in_specs=[anywhere] * 6,
        out_specs=pl.BlockSpec(memory_space=pltpu.VMEM),
        scratch_shapes=[
            pltpu.VMEM((UNITS, tile_len, HALF), jnp.bfloat16),
            pltpu.VMEM((OBS, NX, NY * rows, R), jnp.bfloat16),
            pltpu.VMEM((OBS, NX, R, NY * rows), jnp.bfloat16),
            pltpu.VMEM((OBS, NX, users, NY * rows), jnp.float32),
            pltpu.VMEM((OBS, NX, users, NY * rows), jnp.bfloat16),
            pltpu.VMEM((ITERS, users, R), jnp.float32),
            pltpu.VMEM((ITERS, cols, own, R), jnp.float32),
            pltpu.VMEM((ITERS, cols, own, R), jnp.bfloat16),
            pltpu.VMEM((ITERS, cols, own, R), jnp.bfloat16),
            pltpu.VMEM((cols, own, HALF), jnp.float32),
            pltpu.VMEM((cols, 8, users), jnp.float32),
            pltpu.VMEM((R, R), jnp.float32),
            pltpu.SMEM(tile_counts.shape, jnp.int32),
            pltpu.SMEM(observed_tiles.shape, jnp.int32),
            pltpu.VMEM((1, users), jnp.float32),
            pltpu.VMEM((users, R), jnp.bfloat16),
            pltpu.VMEM(flat.shape, jnp.int32),
            sems((7,)),
            sems((messages,)),
            sems((messages,)),
        ]
        + [sems((ITERS,))] * 6
        + [sems((2,))] * 2,
        compiler_params=pltpu.CompilerParams(
            collective_id=0, has_side_effects=True, vmem_limit_bytes=48 * 2**20
        ),
    )(
        *(
            pltpu.with_memory_space_constraint(array, pltpu.HBM)
            for array in (
                tile_counts,
                observed_tiles,
                confidence.reshape(1, users),
                previous,
                flat,
                item_factors,
            )
        )
    )


def solution(mesh):
    return jax.shard_map(
        local,
        mesh=mesh,
        in_specs=(
            P("col", "row", None),
            P("col"),
            P("row", "col"),
            P("row", "col", None),
            P("row"),
            P("row", None),
        ),
        out_specs=P("row", None),
        check_vma=False,
    )
```

```python
import functools
import heapq
import itertools

import jax
import jax.numpy as jnp
from jax import lax
from jax.experimental import pallas as pl
from jax.experimental.pallas import tpu as pltpu
from jax.sharding import PartitionSpec as P

R = 256
HALF = 128
OBS = 2
ITERS = 3
TILES_COL = 4
UNITS = 2 * TILES_COL
RIDGE = 0.1
NX, NY, NZ = 4, 8, 8
A_UNITS = 5
MESH = pl.DeviceIdType.MESH


SPLIT = 1


def plan(rows):
    unit_us = 1.76 / 5
    costs = {"A": unit_us * A_UNITS, "B": unit_us * (UNITS - A_UNITS)}
    free = {(axis, sign): 0.0 for axis in "xy" for sign in (1, -1)}
    waiting = {link: [] for link in free}
    heap = []
    events = []
    tick = itertools.count()

    def queue(*piece):
        kind, axis, sign, hops, dx, dy = piece[:6]
        turn = -(6 - hops if (kind, axis) in (("A", "y"), ("B", "x")) else (2 if kind == "A" else 4) - hops)
        heapq.heappush(waiting[axis, sign], (turn, next(tick), piece))

    def flush(now, heard):
        order = []
        for link, line in waiting.items():
            while line:
                piece = heapq.heappop(line)[2]
                lo, hi, stride = piece[6:]
                cost = costs[piece[0]] * (hi - lo) / rows
                begin = max(now, free[link])
                free[link] = begin + cost * stride
                heapq.heappush(heap, (begin + cost + 2.5 + 0.5 * stride, next(tick), piece))
                order.append(piece)
        events.append((heard, order, now))

    def spread(kind, axis, dx, dy, lo, hi):
        for stride in (2, 1) if (kind, axis) == ("A", "y") else (1,):
            for sign in (1, -1):
                queue(kind, axis, sign, stride, dx, dy, lo, hi, stride)

    for part in range(SPLIT):
        lo, hi = rows * part // SPLIT, rows * (part + 1) // SPLIT
        for kind, axis in (("A", "y"), ("B", "x"), ("A", "x"), ("B", "y")):
            spread(kind, axis, 0, 0, lo, hi)
    flush(0.0, None)
    while heap:
        now, _, heard = heapq.heappop(heap)
        kind, axis, sign, hops, dx, dy, lo, hi, stride = heard
        last = (NX if axis == "x" else NY) // 2
        if axis == "x":
            dx += sign * stride
        else:
            dy += sign * stride
        if hops < last and not (kind == "A" and axis == "y" and hops == 1):
            middle = (lo + hi) // 2
            if hops < last - 1:
                queue(kind, axis, sign, hops + 1, dx, dy, lo, hi, 1)
            elif sign == 1:
                queue(kind, axis, sign, hops + 1, dx, dy, lo, middle, 1)
            else:
                queue(kind, axis, sign, hops + 1, dx, dy, middle, hi, 1)
        if (kind, axis) == ("A", "y"):
            spread("A", "x", dx, dy, lo, hi)
        if (kind, axis) == ("B", "x"):
            spread("B", "y", dx, dy, lo, hi)
        flush(now, heard)
    return events


def kernel(
    counts_hbm,
    observed_hbm,
    conf_hbm,
    prev_hbm,
    words_hbm,
    item_hbm,
    out_ref,
    buf,
    picked,
    turned,
    cs,
    seen,
    part,
    heard,
    high,
    low,
    steps,
    dots,
    gram,
    gram_other,
    counts,
    observed,
    conf_in,
    prev_in,
    words_in,
    load_sem,
    send_sem,
    recv_sem,
    sum_send,
    sum_recv,
    high_send,
    high_recv,
    low_send,
    low_recv,
    late_send,
    late_recv,
    gram_sem,
    step_sem,
    dot_sem,
    *,
    events,
    rows,
):
    me_row = lax.axis_index("row")
    me_col = lax.axis_index("col")
    my_x, my_y = me_row // NY, me_row % NY
    my_z, my_core = me_col // 2, me_col % 2
    span = NY * rows
    users = prev_in.shape[0]
    cols = 2 * NZ
    own = users // cols

    def at_row(dx, dy):
        return ((my_x + dx + NX) % NX) * NY + (my_y + dy + NY) % NY

    def base_row(row):
        return pl.multiple_of(row * rows, rows)

    partner = my_z * 2 + (1 - my_core)
    peers = []
    same = []
    cross = []
    for dz in sorted(range(NZ), key=lambda d: -min(d, NZ - d)):
        for flip in (0, 1):
            if dz or flip:
                peers.append(((my_z + dz) % NZ) * 2 + (my_core + flip) % 2)
                (cross if flip else same).append(peers[-1])

    mine = base_row(me_row)
    barrier = pltpu.get_barrier_semaphore()
    near = [at_row(1, 0), at_row(-1, 0)] + [at_row(0, d) for d in (1, -1, 2, -2)]
    for row in near:
        pl.semaphore_signal(barrier, inc=1, device_id=(row, me_col), device_id_type=MESH)
    for col in peers:
        pl.semaphore_signal(barrier, inc=1, device_id=(me_row, col), device_id_type=MESH)
    loads = []
    for h in range(2):
        loads.append(
            pltpu.make_async_copy(
                item_hbm.at[:, :, pl.ds(h * HALF, HALF)],
                buf.at[pl.ds(h * TILES_COL, TILES_COL), pl.ds(mine, rows), :],
                load_sem.at[h],
            )
        )
        loads[-1].start()
    others = []
    for i, (src, dst) in enumerate(
        (
            (words_hbm, words_in),
            (counts_hbm, counts),
            (observed_hbm, observed),
            (conf_hbm, conf_in),
            (prev_hbm, prev_in),
        )
    ):
        others.append(pltpu.make_async_copy(src, dst, load_sem.at[2 + i]))
        others[-1].start()

    pl.semaphore_wait(barrier, len(near) + len(peers))
    for load in loads:
        load.wait()

    copies = {}

    def copy_of(piece):
        if piece not in copies:
            kind, axis, sign, _, dx, dy, lo, hi, stride = piece
            units = pl.ds(0, A_UNITS) if kind == "A" else pl.ds(A_UNITS, UNITS - A_UNITS)
            source = base_row(at_row(-dx, -dy))
            place = buf.at[units, pl.ds(source + lo, hi - lo), :]
            target = at_row(sign, 0) if axis == "x" else at_row(0, sign * stride)
            index = len(copies)
            copies[piece] = pltpu.make_async_remote_copy(
                src_ref=place,
                dst_ref=place,
                send_sem=send_sem.at[index],
                recv_sem=recv_sem.at[index],
                device_id=(target, me_col),
                device_id_type=MESH,
            )
        return copies[piece]

    eye = lax.broadcasted_iota(jnp.int32, (users, users), 0) == lax.broadcasted_iota(
        jnp.int32, (users, users), 1
    )

    def column(row):
        return jnp.sum(jnp.where(eye, row, 0.0), axis=1, keepdims=True)

    def expand():
        conf = column(conf_in[...])
        words_wide = words_in.shape[1]
        lanes = 8 * words_wide
        word_of = lax.broadcasted_iota(jnp.int32, (words_wide, lanes), 0)
        slot_of = lax.broadcasted_iota(jnp.int32, (words_wide, lanes), 1)
        scale = 1.0 / jnp.left_shift(1, slot_of & 7).astype(jnp.float32)
        spreader = jnp.where((slot_of >> 3) == word_of, scale, 0.0).astype(jnp.bfloat16)
        for s in range(OBS):
            count = counts[observed[0, s]]
            for half in range(words_in.shape[0] // (users * OBS)):
                words = words_in[pl.ds(half * OBS + s, users, stride=words_in.shape[0] // users), :]
                shifted = jnp.dot(
                    words.astype(jnp.float32).astype(jnp.bfloat16),
                    spreader,
                    preferred_element_type=jnp.float32,
                ).astype(jnp.int32)
                slot = half * lanes + lax.broadcasted_iota(jnp.int32, (users, lanes), 1)
                on = jnp.where(slot < count, shifted & 1, 0).astype(jnp.float32)
                for piece in range(lanes // span):
                    chunk = half * (lanes // span) + piece
                    here = on[:, piece * span : (piece + 1) * span]
                    seen[s, chunk] = here.astype(jnp.bfloat16)
                    cs[s, chunk] = conf * here
        return conf

    def rows_of(tile, chunk):
        place = pl.ds(pl.multiple_of(chunk * span, span), span)
        return jnp.concatenate([buf[tile, place, :], buf[TILES_COL + tile, place, :]], axis=1)

    def weighted(rounded, s, chunk):
        scores = jnp.dot(rounded, turned[s, chunk], preferred_element_type=jnp.float32)
        weights = (cs[s, chunk] * scores).astype(jnp.bfloat16)
        return jnp.dot(weights, picked[s, chunk], preferred_element_type=jnp.float32)

    for piece in events[0][1]:
        copy_of(piece).start()
    for load in others:
        load.wait()
    gram[...] = jnp.zeros_like(gram)
    part[0] = jnp.zeros((users, R), jnp.float32)
    conf = expand()

    def first_pass(chunk):
        slot = chunk * span + lax.broadcasted_iota(jnp.int32, (span, R), 0)
        choice = [None] * OBS
        total = gram[...]
        for tile in range(TILES_COL):
            items = rows_of(tile, chunk)
            for s in range(OBS):
                choice[s] = (
                    items if tile == 0 else jnp.where(observed[0, s] == tile, items, choice[s])
                )
            valid = jnp.where(slot < counts[tile], 1.0, 0.0).astype(jnp.bfloat16)
            total = total + lax.dot_general(
                valid * items, items, (((0,), (0,)), ((), ())), preferred_element_type=jnp.float32
            )
        gram[...] = total
        sums = part[0]
        for s in range(OBS):
            picked[s, chunk] = choice[s]
            turned[s, chunk] = choice[s].T
            sums = sums + (1.0 + conf) * jnp.dot(
                seen[s, chunk], choice[s], preferred_element_type=jnp.float32
            )
            sums = sums - weighted(prev_in[...], s, chunk)
        part[0] = sums

    done = {}
    for index, (piece, _, _) in enumerate(events[1:]):
        _, axis, sign, _, dx, _, _, _, stride = piece
        done[(-dx - (sign * stride if axis == "x" else 0)) % NX] = index
    passed = max(index for index, (_, follow, _) in enumerate(events[1:]) if follow)
    for index, (piece, follow, _) in enumerate(events[1:]):
        copy_of(piece).wait_recv()
        for other in follow:
            copy_of(other).start()
        for dx in range(NX):
            if max(done[dx], passed) == index:
                first_pass((my_x + dx) % NX)

    waits = []

    def finish(ref, sem):
        pltpu.make_async_copy(ref, ref, sem).wait()

    def to_peers(place, send, recv, those):
        for col in those:
            pltpu.make_async_remote_copy(
                src_ref=place.at[me_col],
                dst_ref=place.at[me_col],
                send_sem=send,
                recv_sem=recv,
                device_id=(me_row, col),
                device_id_type=MESH,
            ).start()
        waits.append((place.at[pl.ds(0, len(those))], send))

    def with_gram(vector, matrix):
        return jnp.dot(
            vector,
            matrix,
            precision=lax.Precision.HIGHEST,
            preferred_element_type=jnp.float32,
        )

    def send_sums(k):
        for col in peers:
            pltpu.make_async_remote_copy(
                src_ref=part.at[k, pl.ds(pl.multiple_of(col * own, own), own), :],
                dst_ref=heard.at[k, me_col],
                send_sem=sum_send.at[k],
                recv_sem=sum_recv.at[k],
                device_id=(me_row, col),
                device_id_type=MESH,
            ).start()
        heard[k, me_col] = part[k, pl.ds(pl.multiple_of(me_col * own, own), own), :]
        waits.append((heard.at[k, pl.ds(0, cols - 1)], sum_send.at[k]))

    def take_sums(k):
        finish(heard.at[k, pl.ds(0, cols - 1)], sum_recv.at[k])
        total = heard[k, 0]
        for col in range(1, cols):
            total = total + heard[k, col]
        return total

    def whole(ref, k):
        return ref[k].astype(jnp.float32).reshape(users, R)

    start = prev_in[...].astype(jnp.float32)
    part[0] = part[0] - with_gram(start, gram[...])
    mine_users = (
        lax.broadcasted_iota(jnp.int32, (own, users), 1)
        == me_col * own + lax.broadcasted_iota(jnp.int32, (own, users), 0)
    ).astype(jnp.float32).astype(jnp.bfloat16)
    send_sums(0)
    trade = pltpu.make_async_remote_copy(
        src_ref=gram,
        dst_ref=gram_other,
        send_sem=gram_sem.at[0],
        recv_sem=gram_sem.at[1],
        device_id=(me_row, partner),
        device_id_type=MESH,
    )
    trade.start()
    ours = jnp.dot(mine_users, prev_in[...], preferred_element_type=jnp.float32)
    trade.wait_recv()
    gram_both = gram[...] + gram_other[...]
    residual = take_sums(0) - RIDGE * ours
    direction = residual
    norm_now = jnp.sum(residual * residual, axis=1, keepdims=True)
    lane = lax.broadcasted_iota(jnp.int32, (own, HALF), 1)
    scalars = jnp.zeros((own, HALF), jnp.float32)
    for k in range(ITERS):
        top = direction.astype(jnp.bfloat16)
        rest = (direction - top.astype(jnp.float32)).astype(jnp.bfloat16)
        high[k, me_col] = top
        low[k, me_col] = rest
        to_peers(high.at[k], high_send.at[k], high_recv.at[k], peers)
        if k < ITERS - 1:
            to_peers(low.at[k], low_send.at[k], low_recv.at[k], same)
        else:
            steps[me_col] = jnp.where(lane == k, norm_now, scalars)
            to_peers(steps, step_sem.at[0], step_sem.at[1], peers)
            to_peers(low.at[k], low_send.at[k], low_recv.at[k], same)
            to_peers(low.at[k], late_send.at[k], late_recv.at[k], cross)
        direction = top.astype(jnp.float32) + rest.astype(jnp.float32)
        finish(high.at[k, pl.ds(0, cols - 1)], high_recv.at[k])
        upper = whole(high, k)
        rounded = upper.astype(jnp.bfloat16)
        if k == ITERS - 1:
            break
        sums = jnp.zeros((users, R), jnp.float32)
        for s in range(OBS):
            for chunk in range(NX):
                sums = sums + weighted(rounded, s, chunk)
        place = part.at[k + 1]
        place[...] = sums
        finish(low.at[k, pl.ds(0, len(same))], low_recv.at[k])
        parity = [2 * z + my_core for z in range(NZ)]
        vector = jnp.concatenate(
            [
                high[k, col].astype(jnp.float32) + low[k, col].astype(jnp.float32)
                for col in parity
            ],
            axis=0,
        )
        applied = with_gram(vector, gram_both)
        for z, col in enumerate(parity):
            place[pl.ds(pl.multiple_of(col * own, own), own), :] += applied[z * own : (z + 1) * own]
        send_sums(k + 1)
        to_peers(low.at[k], late_send.at[k], late_recv.at[k], cross)
        image = take_sums(k + 1) + RIDGE * direction
        step_size = norm_now / jnp.sum(direction * image, axis=1, keepdims=True)
        scalars = jnp.where(lane == k, step_size, scalars)
        residual = residual - step_size * image
        norm_next = jnp.sum(residual * residual, axis=1, keepdims=True)
        direction = residual + (norm_next / norm_now) * direction
        norm_now = norm_next

    terms = jnp.zeros((users, span), jnp.float32)
    for s in range(OBS):
        for chunk in range(NX):
            scores = jnp.dot(rounded, turned[s, chunk], preferred_element_type=jnp.float32)
            weights = (cs[s, chunk] * scores).astype(jnp.bfloat16)
            terms = terms + weights.astype(jnp.float32) * scores
    dot_here = jnp.sum(terms, axis=1, keepdims=True) + jnp.sum(
        with_gram(upper, gram[...]) * upper, axis=1, keepdims=True
    )
    dots[me_col] = jnp.broadcast_to(
        jnp.sum(jnp.where(eye, dot_here, 0.0), axis=0, keepdims=True), (8, users)
    )
    to_peers(dots, dot_sem.at[0], dot_sem.at[1], peers)
    finish(steps.at[pl.ds(0, cols - 1)], step_sem.at[1])
    finish(low.at[ITERS - 1, pl.ds(0, len(same))], low_recv.at[ITERS - 1])
    for k in range(ITERS):
        finish(low.at[k, pl.ds(0, len(cross))], late_recv.at[k])
    vector = upper + whole(low, ITERS - 1)
    known = steps[...].reshape(users, HALF)
    answer = start
    for k in range(ITERS - 1):
        answer = answer + known[:, k : k + 1] * (whole(high, k) + whole(low, k))
    ridge = RIDGE * jnp.sum(upper * upper, axis=1, keepdims=True)
    finish(dots.at[pl.ds(0, cols - 1)], dot_sem.at[1])
    total = dots[0, 0:1]
    for col in range(1, cols):
        total = total + dots[col, 0:1]
    step_size = known[:, ITERS - 1 : ITERS] / (column(total) + ridge)
    out_ref[...] = answer + step_size * vector

    for piece in copies:
        copies[piece].wait_send()
    trade.wait_send()
    for several, sem in waits:
        finish(several, sem)


def local(item_factors, tile_counts, observed_tiles, mask_words, confidence, previous):
    rows = item_factors.shape[1]
    users, slots, words = mask_words.shape
    tile_len = NX * NY * rows
    events = plan(rows)
    messages = sum(len(follow) for _, follow, _ in events)
    flat = (
        mask_words.reshape(users, slots, words // HALF, HALF)
        .transpose(0, 2, 1, 3)
        .reshape(users * slots * (words // HALF), HALF)
    )
    anywhere = pl.BlockSpec(memory_space=pltpu.HBM)
    cols = 2 * NZ
    own = users // cols
    sems = pltpu.SemaphoreType.DMA
    return pl.pallas_call(
        functools.partial(kernel, events=events, rows=rows),
        out_shape=jax.ShapeDtypeStruct((users, R), jnp.float32),
        in_specs=[anywhere] * 6,
        out_specs=pl.BlockSpec(memory_space=pltpu.VMEM),
        scratch_shapes=[
            pltpu.VMEM((UNITS, tile_len, HALF), jnp.bfloat16),
            pltpu.VMEM((OBS, NX, NY * rows, R), jnp.bfloat16),
            pltpu.VMEM((OBS, NX, R, NY * rows), jnp.bfloat16),
            pltpu.VMEM((OBS, NX, users, NY * rows), jnp.float32),
            pltpu.VMEM((OBS, NX, users, NY * rows), jnp.bfloat16),
            pltpu.VMEM((ITERS, users, R), jnp.float32),
            pltpu.VMEM((ITERS, cols, own, R), jnp.float32),
            pltpu.VMEM((ITERS, cols, own, R), jnp.bfloat16),
            pltpu.VMEM((ITERS, cols, own, R), jnp.bfloat16),
            pltpu.VMEM((cols, own, HALF), jnp.float32),
            pltpu.VMEM((cols, 8, users), jnp.float32),
            pltpu.VMEM((R, R), jnp.float32),
            pltpu.VMEM((R, R), jnp.float32),
            pltpu.SMEM(tile_counts.shape, jnp.int32),
            pltpu.SMEM(observed_tiles.shape, jnp.int32),
            pltpu.VMEM((1, users), jnp.float32),
            pltpu.VMEM((users, R), jnp.bfloat16),
            pltpu.VMEM(flat.shape, jnp.int32),
            sems((7,)),
            sems((messages,)),
            sems((messages,)),
        ]
        + [sems((ITERS,))] * 8
        + [sems((2,))] * 3,
        compiler_params=pltpu.CompilerParams(
            collective_id=0, has_side_effects=True, vmem_limit_bytes=48 * 2**20
        ),
    )(
        *(
            pltpu.with_memory_space_constraint(array, pltpu.HBM)
            for array in (
                tile_counts,
                observed_tiles,
                confidence.reshape(1, users),
                previous,
                flat,
                item_factors,
            )
        )
    )


def solution(mesh):
    return jax.shard_map(
        local,
        mesh=mesh,
        in_specs=(
            P("col", "row", None),
            P("col"),
            P("row", "col"),
            P("row", "col", None),
            P("row"),
            P("row", None),
        ),
        out_specs=P("row", None),
        check_vma=False,
    )
```

```python
import functools
import heapq
import itertools

import jax
import jax.numpy as jnp
from jax import lax
from jax.experimental import pallas as pl
from jax.experimental.pallas import tpu as pltpu
from jax.sharding import PartitionSpec as P

R = 256
HALF = 128
OBS = 2
ITERS = 3
TILES_COL = 4
UNITS = 2 * TILES_COL
RIDGE = 0.1
NX, NY, NZ = 4, 8, 8
A_UNITS = 5
MESH = pl.DeviceIdType.MESH


SPLIT = 1


def plan(rows):
    unit_us = 1.76 / 5
    costs = {"A": unit_us * A_UNITS, "B": unit_us * (UNITS - A_UNITS)}
    free = {(axis, sign): 0.0 for axis in "xy" for sign in (1, -1)}
    waiting = {link: [] for link in free}
    heap = []
    events = []
    tick = itertools.count()

    def queue(*piece):
        kind, axis, sign, hops, dx, dy = piece[:6]
        turn = -(6 - hops if (kind, axis) in (("A", "y"), ("B", "x")) else (2 if kind == "A" else 4) - hops)
        heapq.heappush(waiting[axis, sign], (turn, next(tick), piece))

    def flush(now, heard):
        order = []
        for link, line in waiting.items():
            while line:
                piece = heapq.heappop(line)[2]
                lo, hi, stride = piece[6:]
                cost = costs[piece[0]] * (hi - lo) / rows
                begin = max(now, free[link])
                free[link] = begin + cost * stride
                heapq.heappush(heap, (begin + cost + 2.5 + 0.5 * stride, next(tick), piece))
                order.append(piece)
        events.append((heard, order, now))

    def spread(kind, axis, dx, dy, lo, hi):
        for stride in (2, 1) if (kind, axis) == ("A", "y") else (1,):
            for sign in (1, -1):
                queue(kind, axis, sign, stride, dx, dy, lo, hi, stride)

    for part in range(SPLIT):
        lo, hi = rows * part // SPLIT, rows * (part + 1) // SPLIT
        for kind, axis in (("A", "y"), ("B", "x"), ("A", "x"), ("B", "y")):
            spread(kind, axis, 0, 0, lo, hi)
    flush(0.0, None)
    while heap:
        now, _, heard = heapq.heappop(heap)
        kind, axis, sign, hops, dx, dy, lo, hi, stride = heard
        last = (NX if axis == "x" else NY) // 2
        if axis == "x":
            dx += sign * stride
        else:
            dy += sign * stride
        if hops < last and not (kind == "A" and axis == "y" and hops == 1):
            middle = (lo + hi) // 2
            if hops < last - 1:
                queue(kind, axis, sign, hops + 1, dx, dy, lo, hi, 1)
            elif sign == 1:
                queue(kind, axis, sign, hops + 1, dx, dy, lo, middle, 1)
            else:
                queue(kind, axis, sign, hops + 1, dx, dy, middle, hi, 1)
        if (kind, axis) == ("A", "y"):
            spread("A", "x", dx, dy, lo, hi)
        if (kind, axis) == ("B", "x"):
            spread("B", "y", dx, dy, lo, hi)
        flush(now, heard)
    return events


def kernel(
    counts_hbm,
    observed_hbm,
    conf_hbm,
    prev_hbm,
    words_hbm,
    item_hbm,
    out_ref,
    buf,
    picked,
    turned,
    cs,
    seen,
    part,
    heard,
    high,
    low,
    steps,
    dots,
    gram,
    gram_other,
    counts,
    observed,
    conf_in,
    prev_in,
    words_in,
    load_sem,
    send_sem,
    recv_sem,
    sum_send,
    sum_recv,
    high_send,
    high_recv,
    low_send,
    low_recv,
    late_send,
    late_recv,
    gram_sem,
    step_sem,
    dot_sem,
    *,
    events,
    rows,
):
    me_row = lax.axis_index("row")
    me_col = lax.axis_index("col")
    my_x, my_y = me_row // NY, me_row % NY
    my_z, my_core = me_col // 2, me_col % 2
    span = NY * rows
    users = prev_in.shape[0]
    cols = 2 * NZ
    own = users // cols

    def at_row(dx, dy):
        return ((my_x + dx + NX) % NX) * NY + (my_y + dy + NY) % NY

    def base_row(row):
        return pl.multiple_of(row * rows, rows)

    partner = my_z * 2 + (1 - my_core)
    peers = []
    same = []
    cross = []
    for dz in sorted(range(NZ), key=lambda d: -min(d, NZ - d)):
        for flip in (0, 1):
            if dz or flip:
                peers.append(((my_z + dz) % NZ) * 2 + (my_core + flip) % 2)
                (cross if flip else same).append(peers[-1])

    mine = base_row(me_row)
    barrier = pltpu.get_barrier_semaphore()
    near = [at_row(1, 0), at_row(-1, 0)] + [at_row(0, d) for d in (1, -1, 2, -2)]
    for row in near:
        pl.semaphore_signal(barrier, inc=1, device_id=(row, me_col), device_id_type=MESH)
    for col in peers:
        pl.semaphore_signal(barrier, inc=1, device_id=(me_row, col), device_id_type=MESH)
    loads = []
    for h in range(2):
        loads.append(
            pltpu.make_async_copy(
                item_hbm.at[:, :, pl.ds(h * HALF, HALF)],
                buf.at[pl.ds(h * TILES_COL, TILES_COL), pl.ds(mine, rows), :],
                load_sem.at[h],
            )
        )
        loads[-1].start()
    others = []
    for i, (src, dst) in enumerate(
        (
            (words_hbm, words_in.at[pl.ds(0, words_hbm.shape[0]), :]),
            (counts_hbm, counts),
            (observed_hbm, observed),
            (conf_hbm, conf_in),
            (prev_hbm, prev_in),
        )
    ):
        others.append(pltpu.make_async_copy(src, dst, load_sem.at[2 + i]))
        others[-1].start()

    pl.semaphore_wait(barrier, len(near) + len(peers))
    for load in loads:
        load.wait()

    copies = {}

    def copy_of(piece):
        if piece not in copies:
            kind, axis, sign, _, dx, dy, lo, hi, stride = piece
            units = pl.ds(0, A_UNITS) if kind == "A" else pl.ds(A_UNITS, UNITS - A_UNITS)
            source = base_row(at_row(-dx, -dy))
            place = buf.at[units, pl.ds(source + lo, hi - lo), :]
            target = at_row(sign, 0) if axis == "x" else at_row(0, sign * stride)
            index = len(copies)
            copies[piece] = pltpu.make_async_remote_copy(
                src_ref=place,
                dst_ref=place,
                send_sem=send_sem.at[index],
                recv_sem=recv_sem.at[index],
                device_id=(target, me_col),
                device_id_type=MESH,
            )
        return copies[piece]

    eye = lax.broadcasted_iota(jnp.int32, (users, users), 0) == lax.broadcasted_iota(
        jnp.int32, (users, users), 1
    )

    def column(row):
        return jnp.sum(jnp.where(eye, row, 0.0), axis=1, keepdims=True)

    def expand():
        conf = column(conf_in[...])
        words_tall, words_wide = words_hbm.shape
        lanes = 8 * words_wide
        word_of = lax.broadcasted_iota(jnp.int32, (words_wide, lanes), 0)
        slot_of = lax.broadcasted_iota(jnp.int32, (words_wide, lanes), 1)
        scale = 1.0 / jnp.left_shift(1, slot_of & 7).astype(jnp.float32)
        spreader = jnp.where((slot_of >> 3) == word_of, scale, 0.0).astype(jnp.bfloat16)
        for s in range(OBS):
            count = counts[observed[0, s]]
            for half in range(words_tall // (users * OBS)):
                words = words_in[pl.ds(half * OBS + s, users, stride=words_tall // users), :]
                shifted = jnp.dot(
                    words.astype(jnp.float32).astype(jnp.bfloat16),
                    spreader,
                    preferred_element_type=jnp.float32,
                ).astype(jnp.int32)
                slot = half * lanes + lax.broadcasted_iota(jnp.int32, (users, lanes), 1)
                on = jnp.where(slot < count, shifted & 1, 0).astype(jnp.float32)
                for piece in range(lanes // span):
                    chunk = half * (lanes // span) + piece
                    here = on[:, piece * span : (piece + 1) * span]
                    seen[s, chunk] = here.astype(jnp.bfloat16)
                    cs[s, chunk] = conf * here
        return conf

    def rows_of(tile, chunk):
        place = pl.ds(pl.multiple_of(chunk * span, span), span)
        return jnp.concatenate([buf[tile, place, :], buf[TILES_COL + tile, place, :]], axis=1)

    def weighted(rounded, s, chunk):
        scores = jnp.dot(rounded, turned[s, chunk], preferred_element_type=jnp.float32)
        weights = (cs[s, chunk] * scores).astype(jnp.bfloat16)
        return jnp.dot(weights, picked[s, chunk], preferred_element_type=jnp.float32)

    for piece in events[0][1]:
        copy_of(piece).start()
    for load in others:
        load.wait()
    gram[...] = jnp.zeros_like(gram)
    part[0] = jnp.zeros((users, R), jnp.float32)
    conf = expand()

    def first_pass(chunk):
        slot = chunk * span + lax.broadcasted_iota(jnp.int32, (span, R), 0)
        choice = [None] * OBS
        total = gram[...]
        for tile in range(TILES_COL):
            items = rows_of(tile, chunk)
            for s in range(OBS):
                choice[s] = (
                    items if tile == 0 else jnp.where(observed[0, s] == tile, items, choice[s])
                )
            valid = jnp.where(slot < counts[tile], 1.0, 0.0).astype(jnp.bfloat16)
            total = total + lax.dot_general(
                valid * items, items, (((0,), (0,)), ((), ())), preferred_element_type=jnp.float32
            )
        gram[...] = total
        sums = part[0]
        for s in range(OBS):
            picked[s, chunk] = choice[s]
            turned[s, chunk] = choice[s].T
            sums = sums + (1.0 + conf) * jnp.dot(
                seen[s, chunk], choice[s], preferred_element_type=jnp.float32
            )
            sums = sums - weighted(prev_in[...], s, chunk)
        part[0] = sums

    done = {}
    for index, (piece, _, _) in enumerate(events[1:]):
        _, axis, sign, _, dx, _, _, _, stride = piece
        done[(-dx - (sign * stride if axis == "x" else 0)) % NX] = index
    passed = max(index for index, (_, follow, _) in enumerate(events[1:]) if follow)
    for index, (piece, follow, _) in enumerate(events[1:]):
        copy_of(piece).wait_recv()
        for other in follow:
            copy_of(other).start()
        for dx in range(NX):
            if max(done[dx], passed) == index:
                first_pass((my_x + dx) % NX)

    waits = []

    def finish(ref, sem):
        pltpu.make_async_copy(ref, ref, sem).wait()

    def to_peers(place, send, recv, those):
        for col in those:
            pltpu.make_async_remote_copy(
                src_ref=place.at[me_col],
                dst_ref=place.at[me_col],
                send_sem=send,
                recv_sem=recv,
                device_id=(me_row, col),
                device_id_type=MESH,
            ).start()
        waits.append((place.at[pl.ds(0, len(those))], send))

    def with_gram(vector, matrix):
        return jnp.dot(
            vector,
            matrix,
            precision=lax.Precision.HIGHEST,
            preferred_element_type=jnp.float32,
        )

    def in_parts(rounded, parts):
        return sum(
            jnp.dot(rounded, part_now, preferred_element_type=jnp.float32) for part_now in parts
        )

    def parts_of(matrix):
        parts = []
        for _ in range(3):
            parts.append(matrix.astype(jnp.bfloat16))
            matrix = matrix - parts[-1].astype(jnp.float32)
        return parts[::-1]

    def send_sums(k):
        for col in peers:
            pltpu.make_async_remote_copy(
                src_ref=part.at[k, pl.ds(pl.multiple_of(col * own, own), own), :],
                dst_ref=heard.at[k, me_col],
                send_sem=sum_send.at[k],
                recv_sem=sum_recv.at[k],
                device_id=(me_row, col),
                device_id_type=MESH,
            ).start()
        heard[k, me_col] = part[k, pl.ds(pl.multiple_of(me_col * own, own), own), :]
        waits.append((heard.at[k, pl.ds(0, cols - 1)], sum_send.at[k]))

    def take_sums(k):
        finish(heard.at[k, pl.ds(0, cols - 1)], sum_recv.at[k])
        total = heard[k, 0]
        for col in range(1, cols):
            total = total + heard[k, col]
        return total

    def whole(ref, k):
        return ref[k].astype(jnp.float32).reshape(users, R)

    start = prev_in[...].astype(jnp.float32)
    gram_parts = parts_of(gram[...])
    part[0] = part[0] - in_parts(prev_in[...], gram_parts)
    mine_users = (
        lax.broadcasted_iota(jnp.int32, (own, users), 1)
        == me_col * own + lax.broadcasted_iota(jnp.int32, (own, users), 0)
    ).astype(jnp.float32).astype(jnp.bfloat16)
    send_sums(0)
    trade = pltpu.make_async_remote_copy(
        src_ref=gram,
        dst_ref=gram_other,
        send_sem=gram_sem.at[0],
        recv_sem=gram_sem.at[1],
        device_id=(me_row, partner),
        device_id_type=MESH,
    )
    trade.start()
    ours = jnp.dot(mine_users, prev_in[...], preferred_element_type=jnp.float32)
    trade.wait_recv()
    gram_both = gram[...] + gram_other[...]
    residual = take_sums(0) - RIDGE * ours
    direction = residual
    norm_now = jnp.sum(residual * residual, axis=1, keepdims=True)
    lane = lax.broadcasted_iota(jnp.int32, (own, HALF), 1)
    scalars = jnp.zeros((own, HALF), jnp.float32)
    for k in range(ITERS):
        top = direction.astype(jnp.bfloat16)
        rest = (direction - top.astype(jnp.float32)).astype(jnp.bfloat16)
        high[k, me_col] = top
        low[k, me_col] = rest
        to_peers(high.at[k], high_send.at[k], high_recv.at[k], peers)
        if k < ITERS - 1:
            to_peers(low.at[k], low_send.at[k], low_recv.at[k], same)
        else:
            steps[me_col] = jnp.where(lane == k, norm_now, scalars)
            to_peers(steps, step_sem.at[0], step_sem.at[1], peers)
            to_peers(low.at[k], low_send.at[k], low_recv.at[k], same)
            to_peers(low.at[k], late_send.at[k], late_recv.at[k], cross)
        direction = top.astype(jnp.float32) + rest.astype(jnp.float32)
        finish(high.at[k, pl.ds(0, cols - 1)], high_recv.at[k])
        upper = whole(high, k)
        rounded = upper.astype(jnp.bfloat16)
        if k == ITERS - 1:
            break
        sums = jnp.zeros((users, R), jnp.float32)
        for s in range(OBS):
            for chunk in range(NX):
                sums = sums + weighted(rounded, s, chunk)
        place = part.at[k + 1]
        place[...] = sums
        finish(low.at[k, pl.ds(0, len(same))], low_recv.at[k])
        parity = [2 * z + my_core for z in range(NZ)]
        vector = jnp.concatenate(
            [
                high[k, col].astype(jnp.float32) + low[k, col].astype(jnp.float32)
                for col in parity
            ],
            axis=0,
        )
        applied = with_gram(vector, gram_both)
        for z, col in enumerate(parity):
            place[pl.ds(pl.multiple_of(col * own, own), own), :] += applied[z * own : (z + 1) * own]
        send_sums(k + 1)
        to_peers(low.at[k], late_send.at[k], late_recv.at[k], cross)
        image = take_sums(k + 1) + RIDGE * direction
        step_size = norm_now / jnp.sum(direction * image, axis=1, keepdims=True)
        scalars = jnp.where(lane == k, step_size, scalars)
        residual = residual - step_size * image
        norm_next = jnp.sum(residual * residual, axis=1, keepdims=True)
        direction = residual + (norm_next / norm_now) * direction
        norm_now = norm_next

    terms = jnp.zeros((users, span), jnp.float32)
    for s in range(OBS):
        for chunk in range(NX):
            scores = jnp.dot(rounded, turned[s, chunk], preferred_element_type=jnp.float32)
            weights = (cs[s, chunk] * scores).astype(jnp.bfloat16)
            terms = terms + weights.astype(jnp.float32) * scores
    dot_here = jnp.sum(terms, axis=1, keepdims=True) + jnp.sum(
        in_parts(rounded, gram_parts) * upper, axis=1, keepdims=True
    )
    dots[me_col] = jnp.broadcast_to(
        jnp.sum(jnp.where(eye, dot_here, 0.0), axis=0, keepdims=True), (8, users)
    )
    to_peers(dots, dot_sem.at[0], dot_sem.at[1], peers)
    finish(steps.at[pl.ds(0, cols - 1)], step_sem.at[1])
    finish(low.at[ITERS - 1, pl.ds(0, len(same))], low_recv.at[ITERS - 1])
    for k in range(ITERS):
        finish(low.at[k, pl.ds(0, len(cross))], late_recv.at[k])
    vector = upper + whole(low, ITERS - 1)
    known = steps[...].reshape(users, HALF)
    answer = start
    for k in range(ITERS - 1):
        answer = answer + known[:, k : k + 1] * (whole(high, k) + whole(low, k))
    ridge = RIDGE * jnp.sum(upper * upper, axis=1, keepdims=True)
    finish(dots.at[pl.ds(0, cols - 1)], dot_sem.at[1])
    total = dots[0, 0:1]
    for col in range(1, cols):
        total = total + dots[col, 0:1]
    step_size = known[:, ITERS - 1 : ITERS] / (column(total) + ridge)
    out_ref[...] = answer + step_size * vector

    for piece in copies:
        copies[piece].wait_send()
    trade.wait_send()
    for several, sem in waits:
        finish(several, sem)


def local(item_factors, tile_counts, observed_tiles, mask_words, confidence, previous):
    rows = item_factors.shape[1]
    users, slots, words = mask_words.shape
    tile_len = NX * NY * rows
    events = plan(rows)
    messages = sum(len(follow) for _, follow, _ in events)
    flat = (
        mask_words.reshape(users, slots, words // HALF, HALF)
        .transpose(0, 2, 1, 3)
        .reshape(users * slots * (words // HALF), HALF)
    )
    anywhere = pl.BlockSpec(memory_space=pltpu.HBM)
    cols = 2 * NZ
    own = users // cols
    sems = pltpu.SemaphoreType.DMA
    return pl.pallas_call(
        functools.partial(kernel, events=events, rows=rows),
        out_shape=jax.ShapeDtypeStruct((users, R), jnp.float32),
        in_specs=[anywhere] * 6,
        out_specs=pl.BlockSpec(memory_space=pltpu.VMEM),
        scratch_shapes=[
            pltpu.VMEM((UNITS, tile_len, HALF), jnp.bfloat16),
            pltpu.VMEM((OBS, NX, NY * rows, R), jnp.bfloat16),
            pltpu.VMEM((OBS, NX, R, NY * rows), jnp.bfloat16),
            pltpu.VMEM((OBS, NX, users, NY * rows), jnp.float32),
            pltpu.VMEM((OBS, NX, users, NY * rows), jnp.bfloat16),
            pltpu.VMEM((ITERS, users, R), jnp.float32),
            pltpu.VMEM((ITERS, cols, own, R), jnp.float32),
            pltpu.VMEM((ITERS, cols, own, R), jnp.bfloat16),
            pltpu.VMEM((ITERS, cols, own, R), jnp.bfloat16),
            pltpu.VMEM((cols, own, HALF), jnp.float32),
            pltpu.VMEM((cols, 8, users), jnp.float32),
            pltpu.VMEM((R, R), jnp.float32),
            pltpu.VMEM((R, R), jnp.float32),
            pltpu.SMEM(tile_counts.shape, jnp.int32),
            pltpu.SMEM(observed_tiles.shape, jnp.int32),
            pltpu.VMEM((1, users), jnp.float32),
            pltpu.VMEM((users, R), jnp.bfloat16),
            pltpu.VMEM((flat.shape[0] + 8, HALF), jnp.int32),
            sems((7,)),
            sems((messages,)),
            sems((messages,)),
        ]
        + [sems((ITERS,))] * 8
        + [sems((2,))] * 3,
        compiler_params=pltpu.CompilerParams(
            collective_id=0, has_side_effects=True, vmem_limit_bytes=48 * 2**20
        ),
    )(
        *(
            pltpu.with_memory_space_constraint(array, pltpu.HBM)
            for array in (
                tile_counts,
                observed_tiles,
                confidence.reshape(1, users),
                previous,
                flat,
                item_factors,
            )
        )
    )


def solution(mesh):
    return jax.shard_map(
        local,
        mesh=mesh,
        in_specs=(
            P("col", "row", None),
            P("col"),
            P("row", "col"),
            P("row", "col", None),
            P("row"),
            P("row", None),
        ),
        out_specs=P("row", None),
        check_vma=False,
    )
```

```python
import functools
import heapq
import itertools

import jax
import jax.numpy as jnp
from jax import lax
from jax.experimental import pallas as pl
from jax.experimental.pallas import tpu as pltpu
from jax.sharding import PartitionSpec as P

R = 256
HALF = 128
OBS = 2
ITERS = 3
TILES_COL = 4
UNITS = 2 * TILES_COL
RIDGE = 0.1
NX, NY, NZ = 4, 8, 8
A_UNITS = 5
MESH = pl.DeviceIdType.MESH


SPLIT = 1


def plan(rows):
    unit_us = 1.76 / 5
    costs = {"A": unit_us * A_UNITS, "B": unit_us * (UNITS - A_UNITS)}
    free = {(axis, sign): 0.0 for axis in "xy" for sign in (1, -1)}
    waiting = {link: [] for link in free}
    heap = []
    events = []
    tick = itertools.count()

    def queue(*piece):
        kind, axis, sign, hops, dx, dy = piece[:6]
        turn = -(6 - hops if (kind, axis) in (("A", "y"), ("B", "x")) else (2 if kind == "A" else 4) - hops)
        heapq.heappush(waiting[axis, sign], (turn, next(tick), piece))

    def flush(now, heard):
        order = []
        for link, line in waiting.items():
            while line:
                piece = heapq.heappop(line)[2]
                lo, hi, stride = piece[6:]
                cost = costs[piece[0]] * (hi - lo) / rows
                begin = max(now, free[link])
                free[link] = begin + cost * stride
                heapq.heappush(heap, (begin + cost + 2.5 + 0.5 * stride, next(tick), piece))
                order.append(piece)
        events.append((heard, order, now))

    def spread(kind, axis, dx, dy, lo, hi):
        for stride in (2, 1) if (kind, axis) == ("A", "y") else (1,):
            for sign in (1, -1):
                queue(kind, axis, sign, stride, dx, dy, lo, hi, stride)

    for part in range(SPLIT):
        lo, hi = rows * part // SPLIT, rows * (part + 1) // SPLIT
        for kind, axis in (("A", "y"), ("B", "x"), ("A", "x"), ("B", "y")):
            spread(kind, axis, 0, 0, lo, hi)
    flush(0.0, None)
    while heap:
        now, _, heard = heapq.heappop(heap)
        kind, axis, sign, hops, dx, dy, lo, hi, stride = heard
        last = (NX if axis == "x" else NY) // 2
        if axis == "x":
            dx += sign * stride
        else:
            dy += sign * stride
        if hops < last and not (kind == "A" and axis == "y" and hops == 1):
            middle = (lo + hi) // 2
            if hops < last - 1:
                queue(kind, axis, sign, hops + 1, dx, dy, lo, hi, 1)
            elif sign == 1:
                queue(kind, axis, sign, hops + 1, dx, dy, lo, middle, 1)
            else:
                queue(kind, axis, sign, hops + 1, dx, dy, middle, hi, 1)
        if (kind, axis) == ("A", "y"):
            spread("A", "x", dx, dy, lo, hi)
        if (kind, axis) == ("B", "x"):
            spread("B", "y", dx, dy, lo, hi)
        flush(now, heard)
    return events


def kernel(
    counts_hbm,
    observed_hbm,
    conf_hbm,
    prev_hbm,
    words_hbm,
    item_hbm,
    out_ref,
    buf,
    picked,
    turned,
    cs,
    seen,
    part,
    heard,
    high,
    low,
    steps,
    dots,
    gram,
    gram_other,
    counts,
    observed,
    conf_in,
    prev_in,
    words_in,
    load_sem,
    send_sem,
    recv_sem,
    sum_send,
    sum_recv,
    high_send,
    high_recv,
    low_send,
    low_recv,
    late_send,
    late_recv,
    gram_sem,
    step_sem,
    dot_sem,
    *,
    events,
    rows,
):
    me_row = lax.axis_index("row")
    me_col = lax.axis_index("col")
    my_x, my_y = me_row // NY, me_row % NY
    my_z, my_core = me_col // 2, me_col % 2
    span = NY * rows
    users = prev_in.shape[0]
    cols = 2 * NZ
    own = users // cols

    def at_row(dx, dy):
        return ((my_x + dx + NX) % NX) * NY + (my_y + dy + NY) % NY

    def base_row(row):
        return pl.multiple_of(row * rows, rows)

    partner = my_z * 2 + (1 - my_core)
    peers = []
    same = []
    cross = []
    for dz in sorted(range(NZ), key=lambda d: -min(d, NZ - d)):
        for flip in (0, 1):
            if dz or flip:
                peers.append(((my_z + dz) % NZ) * 2 + (my_core + flip) % 2)
                (cross if flip else same).append(peers[-1])

    mine = base_row(me_row)
    barrier = pltpu.get_barrier_semaphore()
    near = [at_row(1, 0), at_row(-1, 0)] + [at_row(0, d) for d in (1, -1, 2, -2)]
    for row in near:
        pl.semaphore_signal(barrier, inc=1, device_id=(row, me_col), device_id_type=MESH)
    for col in peers:
        pl.semaphore_signal(barrier, inc=1, device_id=(me_row, col), device_id_type=MESH)
    loads = []
    for h in range(2):
        loads.append(
            pltpu.make_async_copy(
                item_hbm.at[:, :, pl.ds(h * HALF, HALF)],
                buf.at[pl.ds(h * TILES_COL, TILES_COL), pl.ds(mine, rows), :],
                load_sem.at[h],
            )
        )
        loads[-1].start()
    others = []
    for i, (src, dst) in enumerate(
        (
            (words_hbm, words_in.at[pl.ds(0, words_hbm.shape[0]), :]),
            (counts_hbm, counts),
            (observed_hbm, observed),
            (conf_hbm, conf_in),
            (prev_hbm, prev_in),
        )
    ):
        others.append(pltpu.make_async_copy(src, dst, load_sem.at[2 + i]))
        others[-1].start()

    pl.semaphore_wait(barrier, len(near) + len(peers))
    for load in loads:
        load.wait()

    copies = {}

    def copy_of(piece):
        if piece not in copies:
            kind, axis, sign, _, dx, dy, lo, hi, stride = piece
            units = pl.ds(0, A_UNITS) if kind == "A" else pl.ds(A_UNITS, UNITS - A_UNITS)
            source = base_row(at_row(-dx, -dy))
            place = buf.at[units, pl.ds(source + lo, hi - lo), :]
            target = at_row(sign, 0) if axis == "x" else at_row(0, sign * stride)
            index = len(copies)
            copies[piece] = pltpu.make_async_remote_copy(
                src_ref=place,
                dst_ref=place,
                send_sem=send_sem.at[index],
                recv_sem=recv_sem.at[index],
                device_id=(target, me_col),
                device_id_type=MESH,
            )
        return copies[piece]

    eye = lax.broadcasted_iota(jnp.int32, (users, users), 0) == lax.broadcasted_iota(
        jnp.int32, (users, users), 1
    )

    def column(row):
        return jnp.sum(jnp.where(eye, row, 0.0), axis=1, keepdims=True)

    def expand():
        conf = column(conf_in[...])
        words_tall, words_wide = words_hbm.shape
        lanes = 8 * words_wide
        word_of = lax.broadcasted_iota(jnp.int32, (words_wide, lanes), 0)
        slot_of = lax.broadcasted_iota(jnp.int32, (words_wide, lanes), 1)
        scale = 1.0 / jnp.left_shift(1, slot_of & 7).astype(jnp.float32)
        spreader = jnp.where((slot_of >> 3) == word_of, scale, 0.0).astype(jnp.bfloat16)
        for s in range(OBS):
            count = counts[observed[0, s]]
            for half in range(words_tall // (users * OBS)):
                words = words_in[pl.ds(half * OBS + s, users, stride=words_tall // users), :]
                shifted = jnp.dot(
                    words.astype(jnp.float32).astype(jnp.bfloat16),
                    spreader,
                    preferred_element_type=jnp.float32,
                ).astype(jnp.int32)
                slot = half * lanes + lax.broadcasted_iota(jnp.int32, (users, lanes), 1)
                on = jnp.where(slot < count, shifted & 1, 0).astype(jnp.float32)
                for piece in range(lanes // span):
                    chunk = half * (lanes // span) + piece
                    here = on[:, piece * span : (piece + 1) * span]
                    seen[s, chunk] = here.astype(jnp.bfloat16)
                    cs[s, chunk] = conf * here
        return conf

    def rows_of(tile, chunk):
        place = pl.ds(pl.multiple_of(chunk * span, span), span)
        return jnp.concatenate([buf[tile, place, :], buf[TILES_COL + tile, place, :]], axis=1)

    def weighted(rounded, s, chunk):
        scores = jnp.dot(rounded, turned[s, chunk], preferred_element_type=jnp.float32)
        weights = (cs[s, chunk] * scores).astype(jnp.bfloat16)
        return jnp.dot(weights, picked[s, chunk], preferred_element_type=jnp.float32)

    for piece in events[0][1]:
        copy_of(piece).start()
    for load in others:
        load.wait()
    gram[...] = jnp.zeros_like(gram)
    part[0] = jnp.zeros((users, R), jnp.float32)
    conf = expand()

    def first_pass(chunk):
        slot = chunk * span + lax.broadcasted_iota(jnp.int32, (span, R), 0)
        choice = [None] * OBS
        total = gram[...]
        for tile in range(TILES_COL):
            items = rows_of(tile, chunk)
            for s in range(OBS):
                choice[s] = (
                    items if tile == 0 else jnp.where(observed[0, s] == tile, items, choice[s])
                )
            valid = jnp.where(slot < counts[tile], 1.0, 0.0).astype(jnp.bfloat16)
            total = total + lax.dot_general(
                valid * items, items, (((0,), (0,)), ((), ())), preferred_element_type=jnp.float32
            )
        gram[...] = total
        sums = part[0]
        for s in range(OBS):
            picked[s, chunk] = choice[s]
            turned[s, chunk] = choice[s].T
            sums = sums + (1.0 + conf) * jnp.dot(
                seen[s, chunk], choice[s], preferred_element_type=jnp.float32
            )
            sums = sums - weighted(prev_in[...], s, chunk)
        part[0] = sums

    done = {}
    for index, (piece, _, _) in enumerate(events[1:]):
        _, axis, sign, _, dx, _, _, _, stride = piece
        done[(-dx - (sign * stride if axis == "x" else 0)) % NX] = index
    passed = max(index for index, (_, follow, _) in enumerate(events[1:]) if follow)
    for index, (piece, follow, _) in enumerate(events[1:]):
        copy_of(piece).wait_recv()
        for other in follow:
            copy_of(other).start()
        for dx in range(NX):
            if max(done[dx], passed) == index:
                first_pass((my_x + dx) % NX)

    waits = []

    def finish(ref, sem):
        pltpu.make_async_copy(ref, ref, sem).wait()

    def to_peers(place, send, recv, those):
        for col in those:
            pltpu.make_async_remote_copy(
                src_ref=place.at[me_col],
                dst_ref=place.at[me_col],
                send_sem=send,
                recv_sem=recv,
                device_id=(me_row, col),
                device_id_type=MESH,
            ).start()
        waits.append((place.at[pl.ds(0, len(those))], send))

    def with_gram(vector, matrix):
        return jnp.dot(
            vector,
            matrix,
            precision=lax.Precision.HIGHEST,
            preferred_element_type=jnp.float32,
        )

    def in_parts(rounded, parts):
        return sum(
            jnp.dot(rounded, part_now, preferred_element_type=jnp.float32) for part_now in parts
        )

    def parts_of(matrix):
        parts = []
        for _ in range(3):
            parts.append(matrix.astype(jnp.bfloat16))
            matrix = matrix - parts[-1].astype(jnp.float32)
        return parts[::-1]

    def send_sums(k):
        for col in peers:
            pltpu.make_async_remote_copy(
                src_ref=part.at[k, pl.ds(pl.multiple_of(col * own, own), own), :],
                dst_ref=heard.at[k, me_col],
                send_sem=sum_send.at[k],
                recv_sem=sum_recv.at[k],
                device_id=(me_row, col),
                device_id_type=MESH,
            ).start()
        heard[k, me_col] = part[k, pl.ds(pl.multiple_of(me_col * own, own), own), :]
        waits.append((heard.at[k, pl.ds(0, cols - 1)], sum_send.at[k]))

    def take_sums(k):
        finish(heard.at[k, pl.ds(0, cols - 1)], sum_recv.at[k])
        total = heard[k, 0]
        for col in range(1, cols):
            total = total + heard[k, col]
        return total

    def whole(ref, k):
        return ref[k].astype(jnp.float32).reshape(users, R)

    start = prev_in[...].astype(jnp.float32)
    gram_parts = parts_of(gram[...])
    part[0] = part[0] - in_parts(prev_in[...], gram_parts)
    mine_users = (
        lax.broadcasted_iota(jnp.int32, (own, users), 1)
        == me_col * own + lax.broadcasted_iota(jnp.int32, (own, users), 0)
    ).astype(jnp.float32).astype(jnp.bfloat16)
    send_sums(0)
    trade = pltpu.make_async_remote_copy(
        src_ref=gram,
        dst_ref=gram_other,
        send_sem=gram_sem.at[0],
        recv_sem=gram_sem.at[1],
        device_id=(me_row, partner),
        device_id_type=MESH,
    )
    trade.start()
    ours = jnp.dot(mine_users, prev_in[...], preferred_element_type=jnp.float32)
    trade.wait_recv()
    gram_both = gram[...] + gram_other[...]
    residual = take_sums(0) - RIDGE * ours
    direction = residual
    norm_now = jnp.sum(residual * residual, axis=1, keepdims=True)
    lane = lax.broadcasted_iota(jnp.int32, (own, HALF), 1)
    scalars = jnp.zeros((own, HALF), jnp.float32)
    for k in range(ITERS):
        top = direction.astype(jnp.bfloat16)
        rest = (direction - top.astype(jnp.float32)).astype(jnp.bfloat16)
        high[k, me_col] = top
        low[k, me_col] = rest
        to_peers(high.at[k], high_send.at[k], high_recv.at[k], peers)
        if k < ITERS - 1:
            to_peers(low.at[k], low_send.at[k], low_recv.at[k], same)
        else:
            steps[me_col] = jnp.where(lane == k, norm_now, scalars)
            to_peers(steps, step_sem.at[0], step_sem.at[1], peers)
            to_peers(low.at[k], low_send.at[k], low_recv.at[k], same)
            for past in range(ITERS):
                to_peers(low.at[past], late_send.at[past], late_recv.at[past], cross)
        direction = top.astype(jnp.float32) + rest.astype(jnp.float32)
        finish(high.at[k, pl.ds(0, cols - 1)], high_recv.at[k])
        upper = whole(high, k)
        rounded = upper.astype(jnp.bfloat16)
        if k == ITERS - 1:
            break
        sums = jnp.zeros((users, R), jnp.float32)
        for s in range(OBS):
            for chunk in range(NX):
                sums = sums + weighted(rounded, s, chunk)
        place = part.at[k + 1]
        place[...] = sums
        finish(low.at[k, pl.ds(0, len(same))], low_recv.at[k])
        parity = [2 * z + my_core for z in range(NZ)]
        vector = jnp.concatenate(
            [
                high[k, col].astype(jnp.float32) + low[k, col].astype(jnp.float32)
                for col in parity
            ],
            axis=0,
        )
        applied = with_gram(vector, gram_both)
        for z, col in enumerate(parity):
            place[pl.ds(pl.multiple_of(col * own, own), own), :] += applied[z * own : (z + 1) * own]
        send_sums(k + 1)
        image = take_sums(k + 1) + RIDGE * direction
        step_size = norm_now / jnp.sum(direction * image, axis=1, keepdims=True)
        scalars = jnp.where(lane == k, step_size, scalars)
        residual = residual - step_size * image
        norm_next = jnp.sum(residual * residual, axis=1, keepdims=True)
        direction = residual + (norm_next / norm_now) * direction
        norm_now = norm_next

    terms = jnp.zeros((users, span), jnp.float32)
    for s in range(OBS):
        for chunk in range(NX):
            scores = jnp.dot(rounded, turned[s, chunk], preferred_element_type=jnp.float32)
            weights = (cs[s, chunk] * scores).astype(jnp.bfloat16)
            terms = terms + weights.astype(jnp.float32) * scores
    dot_here = jnp.sum(terms, axis=1, keepdims=True) + jnp.sum(
        in_parts(rounded, gram_parts) * upper, axis=1, keepdims=True
    )
    dots[me_col] = jnp.broadcast_to(
        jnp.sum(jnp.where(eye, dot_here, 0.0), axis=0, keepdims=True), (8, users)
    )
    to_peers(dots, dot_sem.at[0], dot_sem.at[1], peers)
    finish(steps.at[pl.ds(0, cols - 1)], step_sem.at[1])
    finish(low.at[ITERS - 1, pl.ds(0, len(same))], low_recv.at[ITERS - 1])
    for k in range(ITERS):
        finish(low.at[k, pl.ds(0, len(cross))], late_recv.at[k])
    vector = upper + whole(low, ITERS - 1)
    known = steps[...].reshape(users, HALF)
    answer = start
    for k in range(ITERS - 1):
        answer = answer + known[:, k : k + 1] * (whole(high, k) + whole(low, k))
    ridge = RIDGE * jnp.sum(upper * upper, axis=1, keepdims=True)
    finish(dots.at[pl.ds(0, cols - 1)], dot_sem.at[1])
    total = dots[0, 0:1]
    for col in range(1, cols):
        total = total + dots[col, 0:1]
    step_size = known[:, ITERS - 1 : ITERS] / (column(total) + ridge)
    out_ref[...] = answer + step_size * vector

    for piece in copies:
        copies[piece].wait_send()
    trade.wait_send()
    for several, sem in waits:
        finish(several, sem)


def local(item_factors, tile_counts, observed_tiles, mask_words, confidence, previous):
    rows = item_factors.shape[1]
    users, slots, words = mask_words.shape
    tile_len = NX * NY * rows
    events = plan(rows)
    messages = sum(len(follow) for _, follow, _ in events)
    flat = (
        mask_words.reshape(users, slots, words // HALF, HALF)
        .transpose(0, 2, 1, 3)
        .reshape(users * slots * (words // HALF), HALF)
    )
    anywhere = pl.BlockSpec(memory_space=pltpu.HBM)
    cols = 2 * NZ
    own = users // cols
    sems = pltpu.SemaphoreType.DMA
    return pl.pallas_call(
        functools.partial(kernel, events=events, rows=rows),
        out_shape=jax.ShapeDtypeStruct((users, R), jnp.float32),
        in_specs=[anywhere] * 6,
        out_specs=pl.BlockSpec(memory_space=pltpu.VMEM),
        scratch_shapes=[
            pltpu.VMEM((UNITS, tile_len, HALF), jnp.bfloat16),
            pltpu.VMEM((OBS, NX, NY * rows, R), jnp.bfloat16),
            pltpu.VMEM((OBS, NX, R, NY * rows), jnp.bfloat16),
            pltpu.VMEM((OBS, NX, users, NY * rows), jnp.float32),
            pltpu.VMEM((OBS, NX, users, NY * rows), jnp.bfloat16),
            pltpu.VMEM((ITERS, users, R), jnp.float32),
            pltpu.VMEM((ITERS, cols, own, R), jnp.float32),
            pltpu.VMEM((ITERS, cols, own, R), jnp.bfloat16),
            pltpu.VMEM((ITERS, cols, own, R), jnp.bfloat16),
            pltpu.VMEM((cols, own, HALF), jnp.float32),
            pltpu.VMEM((cols, 8, users), jnp.float32),
            pltpu.VMEM((R, R), jnp.float32),
            pltpu.VMEM((R, R), jnp.float32),
            pltpu.SMEM(tile_counts.shape, jnp.int32),
            pltpu.SMEM(observed_tiles.shape, jnp.int32),
            pltpu.VMEM((1, users), jnp.float32),
            pltpu.VMEM((users, R), jnp.bfloat16),
            pltpu.VMEM((flat.shape[0] + 8, HALF), jnp.int32),
            sems((7,)),
            sems((messages,)),
            sems((messages,)),
        ]
        + [sems((ITERS,))] * 8
        + [sems((2,))] * 3,
        compiler_params=pltpu.CompilerParams(
            collective_id=0, has_side_effects=True, vmem_limit_bytes=48 * 2**20
        ),
    )(
        *(
            pltpu.with_memory_space_constraint(array, pltpu.HBM)
            for array in (
                tile_counts,
                observed_tiles,
                confidence.reshape(1, users),
                previous,
                flat,
                item_factors,
            )
        )
    )


def solution(mesh):
    return jax.shard_map(
        local,
        mesh=mesh,
        in_specs=(
            P("col", "row", None),
            P("col"),
            P("row", "col"),
            P("row", "col", None),
            P("row"),
            P("row", None),
        ),
        out_specs=P("row", None),
        check_vma=False,
    )
```
